128 devices in a mesh: dp: 16 (over x, z), seq: 8 (over y, core).
Axes of the slice: x: 4, y: 4, z: 4, core: 2. Of those that a mesh axis runs over, the one named last changes fastest.
Arguments:
- waveforms: float32 [256, 40960], P(('dp', 'seq')), may hold values from -6 to 6
- utt_len: int32 [64, 4], P('dp'), may hold values from 5120 to 40960, as said below
- pack_order: int32 [64, 4], P('dp'), may hold values from 0 to 3, each once within a row
- conv_first: float32 [10, 512], replicated, may hold values from -2 to 2
- conv_mid: bfloat16 [4, 3, 512, 512], replicated, may hold values from -0.15625 to 0.15625
- conv_last: bfloat16 [2, 2, 512, 512], replicated, may hold values from -0.1875 to 0.1875
- conv_bias: float32 [7, 512], replicated, may hold values from -3 to 3
- conv_gain: float32 [7, 512], replicated, may hold values from 0.1 to 1.9
- conv_shift: float32 [7, 512], replicated, may hold values from -3 to 3
- proj_gain: float32 [512], replicated, may hold values from 0.1 to 1.9
- proj_shift: float32 [512], replicated, may hold values from -3 to 3
- proj_weight: bfloat16 [512, 1024], replicated, may hold values from -0.25 to 0.25
- proj_bias: float32 [1024], replicated, may hold values from -3 to 3
- conf_gain: float32 [2, 1024], replicated, may hold values from 0.1 to 1.9
- conf_up: bfloat16 [2, 1024, 2048], replicated, may hold values from -0.1875 to 0.1875
- conf_depth: float32 [2, 31, 1024], replicated, may hold values from -1 to 1
- depth_bias: float32 [2, 1024], replicated, may hold values from -3 to 3
- conf_down: bfloat16 [2, 1024, 1024], replicated, may hold values from -0.1875 to 0.1875
Outputs:
- encoded: bfloat16 [64, 512, 1024], P('dp', 'seq')
The draws below stay inside these ranges and needn't reach their ends.
Inputs may be any that keep to these rules, and one draw needn't show every extreme that they name: `utt_len`: valid samples of each slot; in every draw some slot has exactly 40960. `pack_order`: each row lists 0 to 3 once.
All inputs are finite; a program needn't handle non-finite values.
Results may differ from the reference program's by a relative error of at most 0.02.
Values may be sent and summed in bfloat16 or wider, within the bound.
A program may use at most 128 MiB of HBM per device.

```python
import jax
import jax.numpy as jnp
from jax import lax

C = 512
D = 1024
KS = 31
HALF = 15
K = 4
LAYERS = 2
UTT_MAX = 40960
F = 512
ROWS = 64
UTTS = 256
SHARE = 1
N_DP = 16


def draw_utt_len(key, part):
    lengths = jax.random.randint(key, (ROWS, K), UTT_MAX // 8, UTT_MAX + 1, dtype=jnp.int32)
    chosen_slot = jax.random.randint(jax.random.fold_in(key, 7), (), 0, ROWS * K, dtype=jnp.int32)
    flat_lengths = lengths.reshape(-1)
    flat_lengths = flat_lengths.at[chosen_slot].set(UTT_MAX)
    return flat_lengths.reshape(ROWS, K)


def levels(key, dims, split, low, high):
    def one(axis_at, shards_of):
        draws = jax.random.uniform(jax.random.fold_in(jax.random.fold_in(key, 6), axis_at), (shards_of,), jnp.float32, low / len(split), high / len(split))
        return jnp.repeat(jnp.exp(draws), dims[axis_at] // shards_of).reshape((-1,) + (1,) * (len(dims) - axis_at - 1))

    loudness = one(*split[0])
    for cut in split[1:]:
        loudness = loudness * one(*cut)
    return loudness


def normal_values(rng, dims, width, most, cuts=(), held_as=jnp.bfloat16):
    values = jax.random.normal(rng, dims, jnp.float32) * width
    if len(cuts) > 0:
        values = levels(rng, dims, cuts, -0.22, 0.18) * values
    return jnp.clip(values, min=-most, max=most).astype(held_as)


def setup_inputs(seed: int = 0) -> dict:
    streams_of = jax.random.split(jax.random.key(seed), 19)
    waveforms = normal_values(streams_of[0], (UTTS, UTT_MAX), 1.0, 6.0, ((0, 128),), jnp.float32)
    utt_len = draw_utt_len(jax.random.fold_in(streams_of[18], 71), 0)
    pack_order = jax.vmap(lambda own: jax.random.permutation(own, K))(jax.random.split(streams_of[2], ROWS)).reshape((ROWS, K)).astype(jnp.int32)
    conv_first = normal_values(streams_of[3], (10, C), 10 ** -0.5, 2.0, (), jnp.float32)
    conv_mid = normal_values(streams_of[4], (4, 3, C, C), (3 * C) ** -0.5, 0.15625)
    conv_last = normal_values(streams_of[5], (2, 2, C, C), (2 * C) ** -0.5, 0.1875)
    conv_bias = normal_values(streams_of[6], (7, C), 0.5, 3.0, (), jnp.float32)
    conv_gain = jnp.clip(1.0 + 0.18 * jax.random.normal(streams_of[7], (7, C), jnp.float32), 0.1, 1.9)
    conv_shift = normal_values(streams_of[8], (7, C), 0.5, 3.0, (), jnp.float32)
    proj_gain = jnp.clip(1.0 + 0.18 * jax.random.normal(streams_of[9], (C,), jnp.float32), 0.1, 1.9)
    proj_shift = normal_values(streams_of[10], (C,), 0.5, 3.0, (), jnp.float32)
    proj_weight = normal_values(streams_of[11], (C, D), C ** -0.5, 0.25)
    proj_bias = normal_values(streams_of[12], (D,), 0.5, 3.0, (), jnp.float32)
    conf_gain = jnp.clip(1.0 + 0.18 * jax.random.normal(streams_of[13], (LAYERS, D), jnp.float32), 0.1, 1.9)
    conf_up = normal_values(streams_of[14], (LAYERS, D, 2 * D), D ** -0.5, 0.1875)
    conf_depth = normal_values(streams_of[15], (LAYERS, KS, D), KS ** -0.5, 1.0, (), jnp.float32)
    depth_bias = normal_values(streams_of[16], (LAYERS, D), 0.5, 3.0, (), jnp.float32)
    conf_down = normal_values(streams_of[17], (LAYERS, D, D), D ** -0.5, 0.1875)
    return {"waveforms": waveforms, "utt_len": utt_len, "pack_order": pack_order, "conv_first": conv_first, "conv_mid": conv_mid, "conv_last": conv_last, "conv_bias": conv_bias, "conv_gain": conv_gain, "conv_shift": conv_shift, "proj_gain": proj_gain, "proj_shift": proj_shift, "proj_weight": proj_weight, "proj_bias": proj_bias, "conf_gain": conf_gain, "conf_up": conf_up, "conf_depth": conf_depth, "depth_bias": depth_bias, "conf_down": conf_down}


EPS = 1e-05

def normalize(values):
    average = lax.optimization_barrier(jnp.mean(values, axis=-1, keepdims=True))
    centred = values - average
    variance = lax.optimization_barrier(jnp.mean(centred * centred, axis=-1, keepdims=True))
    return centred * lax.rsqrt(variance + EPS)

def assemble(utt_block, len_block, order_row):
    utt_count = utt_block.shape[0]
    utt_span = utt_block.shape[1]
    total_len = utt_count * utt_span + 80
    slot_ids = jnp.arange(utt_count, dtype=jnp.int32)
    sample_ids = jnp.arange(utt_span, dtype=jnp.int32)
    packed = jnp.zeros((total_len,), jnp.float32)
    offset = jnp.zeros((), jnp.int32)
    for slot_idx in range(utt_count):
        chosen = slot_ids == order_row[slot_idx]
        segment = lax.optimization_barrier(jnp.sum(jnp.where(chosen[:, None], utt_block, 0.0), axis=0))
        seg_len = jnp.sum(jnp.where(chosen, len_block, 0)).astype(jnp.int32)
        segment = jnp.where(sample_ids < seg_len, segment, 0.0).astype(jnp.float32)
        placed = lax.dynamic_update_slice(jnp.zeros((total_len,), jnp.float32), segment, (offset,))
        packed = packed + placed
        offset = (offset + seg_len).astype(jnp.int32)
    return packed

def finish_layer(summed, bias_row, gain_row, shift_row):
    normed = normalize(summed + bias_row) * gain_row + shift_row
    return jax.nn.gelu(normed, approximate=False).astype(jnp.bfloat16)

def encoder(packed, conv_first, conv_mid, conv_last, conv_bias, conv_gain, conv_shift):
    sample_pairs = packed.reshape(-1, 5)
    steps_out = sample_pairs.shape[0] - 1
    summed = jnp.dot(sample_pairs[:steps_out], conv_first[:5], precision=lax.Precision.HIGHEST, preferred_element_type=jnp.float32)
    summed = summed + jnp.dot(sample_pairs[1:], conv_first[5:], precision=lax.Precision.HIGHEST, preferred_element_type=jnp.float32)
    hidden = finish_layer(summed, conv_bias[0], conv_gain[0], conv_shift[0])
    for layer_idx in range(4):
        length = hidden.shape[0]
        out_len = (length - 3) // 2 + 1
        even_rows = hidden[0:2 * out_len + 1:2]
        odd_rows = hidden[1:2 * out_len:2]
        mid_weight = conv_mid[layer_idx]
        summed = jnp.dot(even_rows[:out_len], mid_weight[0], preferred_element_type=jnp.float32)
        summed = summed + jnp.dot(odd_rows, mid_weight[1], preferred_element_type=jnp.float32)
        summed = summed + jnp.dot(even_rows[1:], mid_weight[2], preferred_element_type=jnp.float32)
        hidden = finish_layer(summed, conv_bias[layer_idx + 1], conv_gain[layer_idx + 1], conv_shift[layer_idx + 1])
    for layer_idx in range(2):
        length = hidden.shape[0]
        out_len = (length - 2) // 2 + 1
        even_rows = hidden[0:2 * out_len:2]
        odd_rows = hidden[1:2 * out_len:2]
        last_weight = conv_last[layer_idx]
        summed = jnp.dot(even_rows, last_weight[0], preferred_element_type=jnp.float32)
        summed = summed + jnp.dot(odd_rows, last_weight[1], preferred_element_type=jnp.float32)
        hidden = finish_layer(summed, conv_bias[layer_idx + 5], conv_gain[layer_idx + 5], conv_shift[layer_idx + 5])
    return hidden

def project(frames, proj_gain, proj_shift, proj_weight, proj_bias):
    row_count, length, channels = frames.shape
    normed = (normalize(frames.astype(jnp.float32)) * proj_gain + proj_shift).astype(jnp.bfloat16)
    projected = jnp.dot(normed.reshape(-1, channels), proj_weight, preferred_element_type=jnp.float32) + proj_bias
    return projected.astype(jnp.bfloat16).reshape(row_count, length, -1)

def lift_gated(stream, gain_row, up_weight, live_mask):
    row_count, length, channels = stream.shape
    lifted = (normalize(stream.astype(jnp.float32)) * gain_row).astype(jnp.bfloat16)
    doubled = jnp.dot(lifted.reshape(-1, channels), up_weight, preferred_element_type=jnp.float32)
    doubled = doubled.reshape(row_count, length, -1)
    gated = doubled[..., :channels] * jax.nn.sigmoid(doubled[..., channels:])
    return jnp.where(live_mask[..., None], gated, 0.0).astype(jnp.bfloat16)

def depth_mix(stream, padded, depth_taps, bias_row, down_weight):
    row_count, length, channels = stream.shape
    summed = jnp.zeros(stream.shape, jnp.float32) + bias_row
    for tap_idx in range(depth_taps.shape[0]):
        summed = summed + padded[:, tap_idx:tap_idx + length, :].astype(jnp.float32) * depth_taps[tap_idx]
    activated = (summed * jax.nn.sigmoid(summed)).astype(jnp.bfloat16)
    branch = jnp.dot(activated.reshape(-1, channels), down_weight, preferred_element_type=jnp.float32)
    return (stream.astype(jnp.float32) + branch.reshape(row_count, length, channels)).astype(jnp.bfloat16)

def reference(waveforms, utt_len, pack_order, conv_first, conv_mid, conv_last, conv_bias, conv_gain, conv_shift, proj_gain, proj_shift, proj_weight, proj_bias, conf_gain, conf_up, conf_depth, depth_bias, conf_down):
    utterances = waveforms.reshape(N_DP, N_DP, SHARE, UTT_MAX).transpose(1, 0, 2, 3).reshape(ROWS, K, UTT_MAX)

    def encode_row(row_items):
        utt_block, len_block, order_row = row_items
        packed = assemble(utt_block, len_block, order_row)
        return encoder(packed, conv_first, conv_mid, conv_last, conv_bias, conv_gain, conv_shift)
    frames = lax.map(encode_row, (utterances, utt_len, pack_order))
    totals = lax.optimization_barrier(jnp.sum(utt_len, axis=1))
    valid_all = ((totals - 400) // 320 + 1).astype(jnp.int32)

    def conform_row(row_items):
        row_frames, row_valid = row_items
        stream = project(row_frames[None], proj_gain, proj_shift, proj_weight, proj_bias)
        positions = jnp.arange(F, dtype=jnp.int32)
        live_mask = (positions < row_valid)[None, :]
        for layer_idx in range(LAYERS):
            gated = lift_gated(stream, conf_gain[layer_idx], conf_up[layer_idx], live_mask)
            padded = jnp.pad(gated, ((0, 0), (HALF, HALF), (0, 0)))
            stream = depth_mix(stream, padded, conf_depth[layer_idx], depth_bias[layer_idx], conf_down[layer_idx])
        return stream[0]
    return lax.map(conform_row, (frames, valid_all))
```

```python
import functools
import jax
import jax.numpy as jnp
from jax import lax
from jax.experimental import pallas as pl
from jax.experimental.pallas import tpu as pltpu
from jax.sharding import PartitionSpec as P

HALF = 15
LAYERS = 2


EPS = 1e-05


def extended(cells, sides, width):
    for axis, dim in sides:
        count = lax.axis_size(axis)
        ends = count - 1
        head = lax.slice_in_dim(cells, 0, width, axis=dim)
        tail = lax.slice_in_dim(cells, cells.shape[dim] - width, cells.shape[dim], axis=dim)
        cells = jnp.concatenate(
            [
                lax.ppermute(tail, axis, [(i, (i + 1) % count) for i in range(ends)]),
                cells,
                lax.ppermute(head, axis, [((i + 1) % count, i) for i in range(ends)]),
            ],
            axis=dim,
        )
    return cells


def normalize(values):
    average = jnp.mean(values, axis=-1, keepdims=True)
    centred = values - average
    variance = jnp.mean(centred * centred, axis=-1, keepdims=True)
    return centred * lax.rsqrt(variance + EPS)


SEG_MAX = 8
NPH = 18
QC = (0.79787296, 0.036364917, -5.735435e-05, -4.7398415e-05, 2.8125112e-06, -5.711017e-08)
QH = tuple(2.0 * c * 4.0 ** i for i, c in enumerate(QC))


def half_gelu(h):
    u = jnp.minimum(h * h, 6.25)
    q = QH[5]
    for c in QH[4::-1]:
        q = q * u + c
    return h + h * jnp.tanh(h * q)


def finish(v, gain, shift):
    ss = jnp.sum(v * v, axis=-1, keepdims=True)
    r = lax.rsqrt(ss * (1.0 / 512) + EPS)
    return half_gelu((v * r) * gain + shift).astype(jnp.bfloat16)


def encoder_kernel(meta, utts, taps, wmid, wlast, bias, gain, shift, out,
                   packed, lhs, y0, y1, e1, e2, e3, e4, e5, e6, out32):
    f32 = jnp.float32
    core = meta[12]
    nv = meta[13]
    packed[...] = jnp.zeros_like(packed)
    lane = lax.broadcasted_iota(jnp.int32, (320, 128), 1)
    sample = lax.broadcasted_iota(jnp.int32, (320, 128), 0) * 128 + lane
    for p in range(4):
        u, off, ln = meta[p], meta[4 + p], meta[8 + p]
        a, b = off // 128, off % 128
        seg = jnp.where(sample < ln, utts[u].astype(f32), 0.0)
        rolled = pltpu.roll(seg, b, 1)
        packed[pl.ds(a, 320), :] += jnp.where(lane >= b, rolled, 0.0)
        packed[pl.ds(a + 1, 320), :] += jnp.where(lane < b, rolled, 0.0)

    def row(ref, l):
        return ref[pl.ds(l, 1), :]

    def dot_(a, b):
        return jnp.dot(a, b, preferred_element_type=f32)

    def epi(y, l, groups, dst, with_bias=True):
        g, s = row(gain, l), row(shift, l)
        b = row(bias, l) if with_bias else None
        for k in range(groups):
            v = y[pl.ds(16 * k, 16), :]
            if with_bias:
                v = v + b
            dst(k, finish(v, g, s))

    def conv3(src, l, start, rows, gap, y):
        y[pl.ds(0, rows), :] = dot_(src[pl.ds(start, rows), :], wmid[l, 0:1024, :]) + dot_(
            src[pl.ds(start + gap, rows), 0:512], wmid[l, 1024:1536, :])

    def put(ref, gap, base=0):
        def at(k, v):
            ref[pl.ds((k // 2) * gap + base, 16), (k % 2) * 512:(k % 2) * 512 + 512] = v
        return at

    def chain(l, x):
        return dot_(x, wmid[l, 0:512, :]) + dot_(x, wmid[l, 512:1024, :]) + dot_(x, wmid[l, 1024:1536, :])
    x = finish(jnp.broadcast_to(row(bias, 0), (16, 512)), row(gain, 0), row(shift, 0))
    for l in range(3):
        x = finish(chain(l, x) + row(bias, l + 1), row(gain, l + 1), row(shift, l + 1))

    def fill(i, _):
        for k in range(NPH):
            e4[pl.ds((k // 2) * 128 + 16 * i, 16), (k % 2) * 512:(k % 2) * 512 + 512] = x
        return 0
    lax.fori_loop(nv, SEG_MAX, fill, 0)

    lane16 = lax.broadcasted_iota(jnp.int32, (16, 128), 1)

    def segment(i, _):
        base = 5 * (32 * i + 16 * core)
        cols = [packed[pl.ds(base + j, 16, stride=5), :] for j in range(6)]
        for q in range(NPH):
            j, o = divmod(40 * q, 128)
            w = cols[j] if o == 0 else pltpu.roll(cols[j], 128 - o, 1)
            if o + 45 > 128:
                w = jnp.where(lane16 < 128 - o, w, pltpu.roll(cols[j + 1], 128 - o, 1))
            w = jnp.where(lane16 >= 126, 1.0, w)
            lhs[pl.ds(16 * q, 16), :] = w.astype(jnp.bfloat16)

        def first(v, y):
            y[...] = dot_(lhs[...], taps[v])

        def put1(j, half):
            def at(q, val):
                e1[pl.ds(pl.multiple_of(64 * q + 16 * j, 16), 16), 512 * half:512 * half + 512] = val
            return at
        first(0, y0)

        def pair(j, _):
            first(2 * j + 1, y1)
            epi(y0, 0, NPH, put1(j, 0), False)
            first(jnp.minimum(2 * j + 2, 7), y0)
            epi(y1, 0, NPH, put1(j, 1), False)
            return 0
        lax.fori_loop(0, 4, pair, 0)

        n = 16 * NPH
        conv3(e1, 0, 0, n, 16, y0)
        conv3(e1, 0, n, n, 16, y1)
        epi(y0, 1, NPH, put(e2, 16, 0))
        conv3(e1, 0, 2 * n, n, 16, y0)
        epi(y1, 1, NPH, put(e2, 16, n // 2))
        conv3(e1, 0, 3 * n, n, 16, y1)
        epi(y0, 1, NPH, put(e2, 16, n))
        conv3(e2, 1, 0, n, 16, y0)
        epi(y1, 1, NPH, put(e2, 16, 3 * n // 2))
        conv3(e2, 1, n, n, 16, y1)
        epi(y0, 2, NPH, put(e3, 16, 0))
        epi(y1, 2, NPH, put(e3, 16, n // 2))
        conv3(e3, 2, 0, n, 16, y0)
        epi(y0, 3, NPH, put(e4, 128, pl.multiple_of(16 * i, 16)))
        return 0
    lax.fori_loop(0, nv, segment, 0)

    def conv2(src, l, start, y):
        y[pl.ds(0, 256), :] = dot_(src[pl.ds(start, 256), :], wlast[l])

    def put8(ref, base):
        def at(k, v):
            ref[pl.ds(base + 16 * (k % 8), 16), (k // 8) * 512:(k // 8) * 512 + 512] = v
        return at
    conv3(e4, 3, 0, 256, 128, y0)
    conv3(e4, 3, 256, 256, 128, y1)
    epi(y0, 4, 16, put8(e5, 0))
    conv3(e4, 3, 512, 256, 128, y0)
    epi(y1, 4, 16, put8(e5, 128))
    conv3(e4, 3, 768, 256, 128, y1)
    epi(y0, 4, 16, put8(e5, 256))
    conv2(e5, 0, 0, y0)
    epi(y1, 4, 16, put8(e5, 384))
    conv2(e5, 0, 256, y1)
    epi(y0, 5, 16, put8(e6, 0))
    epi(y1, 5, 16, put8(e6, 128))
    conv2(e6, 1, 0, y0)

    def last(k, v):
        v = v.astype(f32)
        for c in range(4):
            out32[c, pl.ds(32 * (k % 8) + k // 8, 16, stride=2), :] = v[:, 128 * c:128 * c + 128]
    epi(y0, 6, 16, last)
    for c in range(4):
        out[:, 128 * c:128 * c + 128] = out32[c].astype(jnp.bfloat16)


def prepare(conv_first, conv_mid, conv_last, conv_bias):
    bf16, f32 = jnp.bfloat16, jnp.float32
    def centre(w):
        w = w.astype(f32)
        return w - jnp.mean(w, axis=-1, keepdims=True)
    bias = centre(conv_bias)
    first = centre(conv_first).astype(bf16)
    hi = bias[0].astype(bf16)
    lo = (bias[0] - hi.astype(f32)).astype(bf16)
    tail = jnp.stack([hi, lo])
    taps = jnp.stack([
        jnp.concatenate([jnp.zeros((5 * v, 512), bf16), first, jnp.zeros((116 - 5 * v, 512), bf16), tail])
        for v in range(8)])
    wmid = centre(conv_mid).astype(bf16).reshape(4, 1536, 512)
    wlast = centre(conv_last).astype(bf16).reshape(2, 1024, 512)
    return taps, wmid, wlast, bias


def encode(meta, utts, taps, wmid, wlast, bias, gain, shift):
    bf16, f32 = jnp.bfloat16, jnp.float32
    vm = pl.BlockSpec(memory_space=pltpu.VMEM)
    return pl.pallas_call(
        encoder_kernel,
        out_shape=jax.ShapeDtypeStruct((256, 512), bf16),
        in_specs=[pl.BlockSpec(memory_space=pltpu.SMEM)] + [vm] * 7,
        out_specs=vm,
        scratch_shapes=[
            pltpu.VMEM((1296, 128), f32),
            pltpu.VMEM((288, 128), bf16),
            pltpu.VMEM((288, 512), f32),
            pltpu.VMEM((288, 512), f32),
            pltpu.VMEM((73 * 16, 1024), bf16),
            pltpu.VMEM((37 * 16, 1024), bf16),
            pltpu.VMEM((19 * 16, 1024), bf16),
            pltpu.VMEM((9 * 128, 1024), bf16),
            pltpu.VMEM((4 * 128, 1024), bf16),
            pltpu.VMEM((2 * 128, 1024), bf16),
            pltpu.VMEM((4, 256, 128), f32),
        ],
        compiler_params=pltpu.CompilerParams(vmem_limit_bytes=48 << 20),
        name="encode",
    )(meta, utts, taps, wmid, wlast, bias, gain * 0.5, shift * 0.5)


def project(frames, proj_gain, proj_shift, proj_weight, proj_bias):
    row_count, length, channels = frames.shape
    normed = (normalize(frames.astype(jnp.float32)) * proj_gain + proj_shift).astype(jnp.bfloat16)
    projected = (
        jnp.dot(normed.reshape(-1, channels), proj_weight, preferred_element_type=jnp.float32)
        + proj_bias
    )
    return projected.astype(jnp.bfloat16).reshape(row_count, length, -1)


def lift_gated(stream, gain_row, up_weight, live_mask):
    row_count, length, channels = stream.shape
    lifted = (normalize(stream.astype(jnp.float32)) * gain_row).astype(jnp.bfloat16)
    doubled = jnp.dot(lifted.reshape(-1, channels), up_weight, preferred_element_type=jnp.float32)
    doubled = doubled.reshape(row_count, length, -1)
    gated = doubled[..., :channels] * jax.nn.sigmoid(doubled[..., channels:])
    return jnp.where(live_mask[..., None], gated, 0.0).astype(jnp.bfloat16)


def depth_mix(stream, padded, depth_taps, bias_row, down_weight):
    row_count, length, channels = stream.shape
    summed = jnp.zeros(stream.shape, jnp.float32) + bias_row
    for tap_idx in range(depth_taps.shape[0]):
        summed = (
            summed
            + padded[:, tap_idx : tap_idx + length, :].astype(jnp.float32) * depth_taps[tap_idx]
        )
    activated = (summed * jax.nn.sigmoid(summed)).astype(jnp.bfloat16)
    branch = jnp.dot(
        activated.reshape(-1, channels), down_weight, preferred_element_type=jnp.float32
    )
    return (stream.astype(jnp.float32) + branch.reshape(row_count, length, channels)).astype(
        jnp.bfloat16
    )


def per_device(
    waveforms,
    utt_len,
    pack_order,
    conv_first,
    conv_mid,
    conv_last,
    conv_bias,
    conv_gain,
    conv_shift,
    proj_gain,
    proj_shift,
    proj_weight,
    proj_bias,
    conf_gain,
    conf_up,
    conf_depth,
    depth_bias,
    conf_down,
):
    seq_size = lax.axis_size("seq")
    seq_index = lax.axis_index("seq")
    group_rows = utt_len.shape[0]
    utt_count = utt_len.shape[1]
    utt_span = waveforms.shape[1]
    sharers = seq_size // group_rows
    own_row = seq_index // sharers
    own_part = seq_index % sharers
    across = lax.all_gather(waveforms.astype(jnp.bfloat16), "seq", axis=0, tiled=True).astype(
        waveforms.dtype
    )
    utterances = lax.all_to_all(
        across.astype(jnp.bfloat16), "dp", split_axis=0, concat_axis=0, tiled=True
    ).astype(across.dtype)
    utterances = utterances.reshape(group_rows, utt_count, utt_span)
    row_audio = lax.dynamic_index_in_dim(utterances, own_row, 0, keepdims=False)
    row_frames = utt_count * (utt_span // 320)
    per_shard = row_frames // seq_size
    seg_frames = per_shard // sharers
    row_len = lax.dynamic_index_in_dim(utt_len, own_row, 0, keepdims=False)
    row_order = lax.dynamic_index_in_dim(pack_order, own_row, 0, keepdims=False)
    lens = jnp.sum(jnp.where(row_order[:, None] == jnp.arange(4)[None], row_len[None], 0), axis=1)
    offs = jnp.cumsum(lens) - lens
    total = jnp.sum(lens)
    live = ((total + 10239) // 10240 - own_part + 1) // 2
    meta = jnp.concatenate([row_order, offs, lens, jnp.stack([own_part, live, own_part, own_part])]).astype(jnp.int32)
    segments = encode(
        meta,
        row_audio.reshape(4, 320, 128),
        *prepare(conv_first, conv_mid, conv_last, conv_bias),
        conv_gain,
        conv_shift,
    ).reshape(seq_size, seg_frames, 512)
    outgoing = segments.reshape(seq_size, 1, seg_frames, segments.shape[2])
    received = lax.all_to_all(outgoing, "seq", split_axis=0, concat_axis=1, tiled=True)
    flat_rows = received.reshape(received.shape[1], received.shape[2], received.shape[3])
    projected = project(flat_rows, proj_gain, proj_shift, proj_weight, proj_bias)
    relayed = projected.reshape(1, received.shape[1], received.shape[2], projected.shape[2])
    stream = relayed.reshape(group_rows, per_shard, relayed.shape[3])
    totals = jnp.sum(utt_len, axis=1)
    valid_rows = (totals - 400) // 320 + 1
    positions = seq_index * per_shard + jnp.arange(per_shard, dtype=jnp.int32)
    live_mask = positions[None, :] < valid_rows[:, None]
    for layer_idx in range(LAYERS):
        gated = lift_gated(stream, conf_gain[layer_idx], conf_up[layer_idx], live_mask)
        padded = extended(gated, (("seq", 1),), HALF)
        stream = depth_mix(
            stream, padded, conf_depth[layer_idx], depth_bias[layer_idx], conf_down[layer_idx]
        )
    return stream


def solution(mesh):
    return jax.shard_map(
        per_device,
        mesh=mesh,
        in_specs=(
            P(("dp", "seq"), None),
            P("dp", None),
            P("dp", None),
            P(),
            P(),
            P(),
            P(),
            P(),
            P(),
            P(),
            P(),
            P(),
            P(),
            P(),
            P(),
            P(),
            P(),
            P(),
        ),
        out_specs=P("dp", "seq", None),
        check_vma=False,
    )
```

```python
import jax
import jax.numpy as jnp
from jax import lax
from jax.experimental import pallas as pl
from jax.experimental.pallas import tpu as pltpu
from jax.sharding import PartitionSpec as P

EPS = 1e-05
SEG_MAX = 8
NPH = 18
QC = (0.79787296, 0.036364917, -5.735435e-05, -4.7398415e-05, 2.8125112e-06, -5.711017e-08)
QH = tuple(2.0 * c * 4.0 ** i for i, c in enumerate(QC))


def half_gelu(h):
    u = jnp.minimum(h * h, 6.25)
    q = QH[5]
    for c in QH[4::-1]:
        q = q * u + c
    return h + h * jnp.tanh(h * q)


def finish(v, gain, shift):
    ss = jnp.sum(v * v, axis=-1, keepdims=True)
    r = lax.rsqrt(ss * (1.0 / 512) + EPS)
    return half_gelu((v * r) * gain + shift).astype(jnp.bfloat16)


def encoder_kernel(lens, order, utts, taps, wmid, wlast, bias, gain, shift, pgain, pshift, out,
                   packed, lhs, y0, y1, e1, e2, e3, e4, e5, e6, out32):
    f32 = jnp.float32
    seq = lax.axis_index("seq")
    own, core = seq // 2, seq % 2
    packed[...] = jnp.zeros_like(packed)
    lane = lax.broadcasted_iota(jnp.int32, (320, 128), 1)
    sample = lax.broadcasted_iota(jnp.int32, (320, 128), 0) * 128 + lane
    off = jnp.int32(0)
    for p in range(4):
        u = order[own, p]
        ln = lens[own, u]
        a, b = off // 128, off % 128
        seg = jnp.where(sample < ln, utts[u].astype(f32), 0.0)
        rolled = pltpu.roll(seg, b, 1)
        packed[pl.ds(a, 320), :] += jnp.where(lane >= b, rolled, 0.0)
        packed[pl.ds(a + 1, 320), :] += jnp.where(lane < b, rolled, 0.0)
        off = off + ln
    nv = ((off + 10239) // 10240 - core + 1) // 2

    def row(ref, l):
        return ref[pl.ds(l, 1), :]

    def dot_(a, b):
        return jnp.dot(a, b, preferred_element_type=f32)

    def epi(y, l, groups, dst, with_bias=True):
        g, s = row(gain, l), row(shift, l)
        b = row(bias, l) if with_bias else None
        for k in range(groups):
            v = y[pl.ds(16 * k, 16), :]
            if with_bias:
                v = v + b
            dst(k, finish(v, g, s))

    def conv3(src, l, start, rows, gap, y):
        y[pl.ds(0, rows), :] = dot_(src[pl.ds(start, rows), :], wmid[l, 0:1024, :]) + dot_(
            src[pl.ds(start + gap, rows), 0:512], wmid[l, 1024:1536, :])

    def put(ref, gap, base=0):
        def at(k, v):
            ref[pl.ds((k // 2) * gap + base, 16), (k % 2) * 512:(k % 2) * 512 + 512] = v
        return at

    def chain(l, x):
        return dot_(x, wmid[l, 0:512, :]) + dot_(x, wmid[l, 512:1024, :]) + dot_(x, wmid[l, 1024:1536, :])
    x = finish(jnp.broadcast_to(row(bias, 0), (16, 512)), row(gain, 0), row(shift, 0))
    for l in range(3):
        x = finish(chain(l, x) + row(bias, l + 1), row(gain, l + 1), row(shift, l + 1))

    def fill(i, _):
        for k in range(NPH):
            e4[pl.ds((k // 2) * 128 + 16 * i, 16), (k % 2) * 512:(k % 2) * 512 + 512] = x
        return 0
    lax.fori_loop(nv, SEG_MAX, fill, 0)

    lane16 = lax.broadcasted_iota(jnp.int32, (16, 128), 1)

    def segment(i, _):
        base = 5 * (32 * i + 16 * core)
        cols = [packed[pl.ds(base + j, 16, stride=5), :] for j in range(6)]
        for q in range(NPH):
            j, o = divmod(40 * q, 128)
            w = cols[j] if o == 0 else pltpu.roll(cols[j], 128 - o, 1)
            if o + 45 > 128:
                w = jnp.where(lane16 < 128 - o, w, pltpu.roll(cols[j + 1], 128 - o, 1))
            w = jnp.where(lane16 >= 126, 1.0, w)
            lhs[pl.ds(16 * q, 16), :] = w.astype(jnp.bfloat16)

        def first(v, y):
            y[...] = dot_(lhs[...], taps[v])

        def put1(j, half):
            def at(q, val):
                e1[pl.ds(pl.multiple_of(64 * q + 16 * j, 16), 16), 512 * half:512 * half + 512] = val
            return at
        first(0, y0)

        def pair(j, _):
            first(2 * j + 1, y1)
            epi(y0, 0, NPH, put1(j, 0), False)
            first(jnp.minimum(2 * j + 2, 7), y0)
            epi(y1, 0, NPH, put1(j, 1), False)
            return 0
        lax.fori_loop(0, 4, pair, 0)

        n = 16 * NPH
        conv3(e1, 0, 0, n, 16, y0)
        conv3(e1, 0, n, n, 16, y1)
        epi(y0, 1, NPH, put(e2, 16, 0))
        conv3(e1, 0, 2 * n, n, 16, y0)
        epi(y1, 1, NPH, put(e2, 16, n // 2))
        conv3(e1, 0, 3 * n, n, 16, y1)
        epi(y0, 1, NPH, put(e2, 16, n))
        conv3(e2, 1, 0, n, 16, y0)
        epi(y1, 1, NPH, put(e2, 16, 3 * n // 2))
        conv3(e2, 1, n, n, 16, y1)
        epi(y0, 2, NPH, put(e3, 16, 0))
        epi(y1, 2, NPH, put(e3, 16, n // 2))
        conv3(e3, 2, 0, n, 16, y0)
        epi(y0, 3, NPH, put(e4, 128, pl.multiple_of(16 * i, 16)))
        return 0
    lax.fori_loop(0, nv, segment, 0)

    def conv2(src, l, start, y):
        y[pl.ds(0, 256), :] = dot_(src[pl.ds(start, 256), :], wlast[l])

    def put8(ref, base):
        def at(k, v):
            ref[pl.ds(base + 16 * (k % 8), 16), (k // 8) * 512:(k // 8) * 512 + 512] = v
        return at
    conv3(e4, 3, 0, 256, 128, y0)
    conv3(e4, 3, 256, 256, 128, y1)
    epi(y0, 4, 16, put8(e5, 0))
    conv3(e4, 3, 512, 256, 128, y0)
    epi(y1, 4, 16, put8(e5, 128))
    conv3(e4, 3, 768, 256, 128, y1)
    epi(y0, 4, 16, put8(e5, 256))
    conv2(e5, 0, 0, y0)
    epi(y1, 4, 16, put8(e5, 384))
    conv2(e5, 0, 256, y1)
    epi(y0, 5, 16, put8(e6, 0))
    epi(y1, 5, 16, put8(e6, 128))
    conv2(e6, 1, 0, y0)

    pg, ps = pgain[...], pshift[...]

    def last(k, v):
        v = v.astype(f32)
        v = v - jnp.mean(v, axis=-1, keepdims=True)
        v = v * lax.rsqrt(jnp.mean(v * v, axis=-1, keepdims=True) + EPS) * pg + ps
        for c in range(4):
            out32[c, pl.ds(32 * (k % 8) + k // 8, 16, stride=2), :] = v[:, 128 * c:128 * c + 128]
    epi(y0, 6, 16, last)
    out[0:32, :] = jnp.zeros((32, 512), jnp.bfloat16)
    out[288:320, :] = jnp.zeros((32, 512), jnp.bfloat16)
    for c in range(4):
        out[32:288, 128 * c:128 * c + 128] = out32[c].astype(jnp.bfloat16)


def prepare(conv_first, conv_mid, conv_last, conv_bias):
    bf16, f32 = jnp.bfloat16, jnp.float32
    def centre(w):
        w = w.astype(f32)
        return w - jnp.mean(w, axis=-1, keepdims=True)
    bias = centre(conv_bias)
    first = centre(conv_first).astype(bf16)
    hi = bias[0].astype(bf16)
    lo = (bias[0] - hi.astype(f32)).astype(bf16)
    tail = jnp.stack([hi, lo])
    taps = jnp.stack([
        jnp.concatenate([jnp.zeros((5 * v, 512), bf16), first, jnp.zeros((116 - 5 * v, 512), bf16), tail])
        for v in range(8)])
    wmid = centre(conv_mid).astype(bf16).reshape(4, 1536, 512)
    wlast = centre(conv_last).astype(bf16).reshape(2, 1024, 512)
    return taps, wmid, wlast, bias


def encode(lens, order, utts, taps, wmid, wlast, bias, gain, shift, pgain, pshift):
    bf16, f32 = jnp.bfloat16, jnp.float32
    vm = pl.BlockSpec(memory_space=pltpu.VMEM)
    sm = pl.BlockSpec(memory_space=pltpu.SMEM)
    return pl.pallas_call(
        encoder_kernel,
        out_shape=jax.ShapeDtypeStruct((320, 512), bf16),
        in_specs=[sm, sm] + [vm] * 9,
        out_specs=vm,
        scratch_shapes=[
            pltpu.VMEM((1296, 128), f32),
            pltpu.VMEM((288, 128), bf16),
            pltpu.VMEM((288, 512), f32),
            pltpu.VMEM((288, 512), f32),
            pltpu.VMEM((73 * 16, 1024), bf16),
            pltpu.VMEM((37 * 16, 1024), bf16),
            pltpu.VMEM((19 * 16, 1024), bf16),
            pltpu.VMEM((9 * 128, 1024), bf16),
            pltpu.VMEM((4 * 128, 1024), bf16),
            pltpu.VMEM((2 * 128, 1024), bf16),
            pltpu.VMEM((4, 256, 128), f32),
        ],
        compiler_params=pltpu.CompilerParams(vmem_limit_bytes=40 << 20),
        name="encode",
    )(lens, order, utts, taps, wmid, wlast, bias, gain * 0.5, shift * 0.5, pgain, pshift)


MESH = pl.DeviceIdType.MESH


def audio_kernel(waves, out, stage, held, ssem, rsem):
    dp, seq = lax.axis_index("dp"), lax.axis_index("seq")
    mine = seq == dp // 2
    barrier = pltpu.get_barrier_semaphore()

    def source(k):
        return {"dp": 4 * (seq // 2) + k, "seq": dp // 2}

    for k in range(4):
        @pl.when(jnp.logical_not(jnp.logical_and(mine, dp % 4 == k)))
        def _():
            pl.semaphore_signal(barrier, inc=1, device_id=source(k), device_id_type=MESH)

    def unfold(i, _):
        for e in range(2):
            stage[e, pl.ds(i, 1), :] = waves[e:e + 1, pl.ds(pl.multiple_of(128 * i, 128), 128)]
        return 0
    lax.fori_loop(0, 320, unfold, 0)
    held[...] = stage[...].astype(jnp.bfloat16)
    pl.semaphore_wait(barrier, jnp.where(mine, 3, 4))
    slot = dp % 4

    def copy(e, c):
        return pltpu.make_async_remote_copy(
            src_ref=held.at[e], dst_ref=out.at[slot],
            send_sem=ssem.at[2 * e + c], recv_sem=rsem.at[slot],
            device_id={"dp": 2 * seq + e, "seq": 2 * (dp // 4) + c}, device_id_type=MESH)

    def here(e, c):
        return jnp.logical_and(mine, jnp.logical_and(dp % 2 == e, seq % 2 == c))

    for e in range(2):
        for c in range(2):
            @pl.when(jnp.logical_not(here(e, c)))
            def _():
                copy(e, c).start()

            @pl.when(here(e, c))
            def _():
                out[slot] = held[e]
    for k in range(4):
        @pl.when(jnp.logical_not(jnp.logical_and(mine, slot == k)))
        def _():
            pltpu.make_async_remote_copy(
                src_ref=held.at[0], dst_ref=out.at[k], send_sem=ssem.at[0], recv_sem=rsem.at[k],
                device_id=source(k), device_id_type=MESH).wait_recv()
    for e in range(2):
        for c in range(2):
            @pl.when(jnp.logical_not(here(e, c)))
            def _():
                copy(e, c).wait_send()


def exchange_audio(waves):
    vm = pl.BlockSpec(memory_space=pltpu.VMEM)
    return pl.pallas_call(
        audio_kernel,
        out_shape=jax.ShapeDtypeStruct((4, 320, 128), jnp.bfloat16),
        in_specs=[vm],
        out_specs=vm,
        scratch_shapes=[
            pltpu.VMEM((2, 320, 128), jnp.float32),
            pltpu.VMEM((2, 320, 128), jnp.bfloat16),
            pltpu.SemaphoreType.DMA((4,)),
            pltpu.SemaphoreType.DMA((4,)),
        ],
        compiler_params=pltpu.CompilerParams(collective_id=1, has_side_effects=True),
        name="audio",
    )(waves)


def frames_kernel(frames, out, ssem, rsem):
    seq = lax.axis_index("seq")
    barrier = pltpu.get_barrier_semaphore()
    for o in range(1, 8):
        pl.semaphore_signal(barrier, inc=1, device_id={"seq": (seq + o) % 8}, device_id_type=MESH)

    def piece(d):
        return pl.ds(pl.multiple_of(32 * d + 32 * (1 - seq % 2), 32), 64)

    def copy(o):
        d = (seq + o) % 8
        return pltpu.make_async_remote_copy(
            src_ref=frames.at[piece(d)], dst_ref=out.at[seq],
            send_sem=ssem.at[o], recv_sem=rsem.at[seq],
            device_id={"seq": d}, device_id_type=MESH)
    pl.semaphore_wait(barrier, 7)
    for o in range(1, 8):
        copy(o).start()
    out[seq] = frames[piece(seq), :]
    for o in range(1, 8):
        d = (seq + o) % 8
        pltpu.make_async_remote_copy(
            src_ref=frames.at[piece(d)], dst_ref=out.at[d], send_sem=ssem.at[o], recv_sem=rsem.at[d],
            device_id={"seq": d}, device_id_type=MESH).wait_recv()
    for o in range(1, 8):
        copy(o).wait_send()


def exchange_frames(frames):
    vm = pl.BlockSpec(memory_space=pltpu.VMEM)
    return pl.pallas_call(
        frames_kernel,
        out_shape=jax.ShapeDtypeStruct((8, 64, 512), jnp.bfloat16),
        in_specs=[vm],
        out_specs=vm,
        scratch_shapes=[pltpu.SemaphoreType.DMA((8,)), pltpu.SemaphoreType.DMA((8,))],
        compiler_params=pltpu.CompilerParams(collective_id=2, has_side_effects=True),
        name="frames",
    )(frames)


def conformer_kernel(lens, recv, wp, pb, gain, up, taps, dbias, down, out,
                     nrm, s0, s1, lifted, ya, yb, g, act):
    f32, bf16 = jnp.float32, jnp.bfloat16
    base = 64 * lax.axis_index("seq") - 32
    for r in range(4):
        for c in range(4):
            nrm[128 * r + 32 * c:128 * r + 32 * c + 32, :] = recv[2 * r + (c + 1) % 2, 32 * (c // 2):32 * (c // 2) + 32, :]

    def dot_(a, b):
        return jnp.dot(a, b, preferred_element_type=f32)

    for n in range(4):
        w = slice(256 * n, 256 * n + 256)
        s0[:, w] = dot_(nrm[...], wp[:, w]) + pb[:, w]

    def norm(src, l, rows):
        gl = gain[l:l + 1, :]

        def body(i, _):
            at = pl.ds(pl.multiple_of(16 * i, 16), 16)
            v = src[at, :]
            v = v - jnp.mean(v, axis=-1, keepdims=True)
            v = v * lax.rsqrt(jnp.mean(v * v, axis=-1, keepdims=True) + EPS) * gl
            lifted[at, :] = v.astype(bf16)
            return 0
        lax.fori_loop(0, rows // 16, body, 0, unroll=2)

    def module(l, per, lo, keep):
        rows = 4 * per

        def chunk(n, _):
            wa = pl.ds(pl.multiple_of(256 * n, 256), 256)
            wb = pl.ds(pl.multiple_of(1024 + 256 * n, 256), 256)
            ya[0:rows, :] = dot_(lifted[0:rows, :], up[l, :, wa])
            yb[0:rows, :] = dot_(lifted[0:rows, :], up[l, :, wb])
            for r in range(4):
                total = lens[r, 0] + lens[r, 1] + lens[r, 2] + lens[r, 3]
                valid = (total - 400) // 320 + 1
                for k in range(per // 16):
                    at = slice(per * r + 16 * k, per * r + 16 * k + 16)
                    t = base + lo + 16 * k + lax.broadcasted_iota(jnp.int32, (16, 256), 0)
                    live = jnp.logical_and(t >= 0, t < valid)
                    v = jnp.where(live, ya[at, :] * jax.nn.sigmoid(yb[at, :]), 0.0)
                    g[2 * n, r, lo + 16 * k:lo + 16 * k + 16, :] = v[:, 0:128]
                    g[2 * n + 1, r, lo + 16 * k:lo + 16 * k + 16, :] = v[:, 128:256]
            return 0
        lax.fori_loop(0, 4, chunk, 0)
        first = 64 - keep // 2

        def depth(c, _):
            w = pl.ds(pl.multiple_of(128 * c, 128), 128)

            def one(r, _):
                acc = jnp.broadcast_to(dbias[l:l + 1, w], (keep, 128))
                for j in range(31):
                    acc = acc + g[c, r, first + j - 15:first + j - 15 + keep, :] * taps[l, j:j + 1, w]
                act[pl.ds(pl.multiple_of(keep * r, 32), keep), w] = (acc * jax.nn.sigmoid(acc)).astype(bf16)
                return 0
            return lax.fori_loop(0, 4, one, 0)
        lax.fori_loop(0, 8, depth, 0)

    norm(s0, 0, 512)
    module(0, 128, 0, 96)
    for n in range(4):
        w = slice(256 * n, 256 * n + 256)
        d = dot_(act[...], down[0, :, w])
        for r in range(4):
            s1[96 * r:96 * r + 96, w] = s0[128 * r + 16:128 * r + 112, w] + d[96 * r:96 * r + 96]
    norm(s1, 1, 384)
    module(1, 96, 16, 64)
    for n in range(4):
        w = slice(256 * n, 256 * n + 256)
        d = dot_(act[0:256, :], down[1, :, w])
        for r in range(4):
            out[r, :, w] = (s1[96 * r + 16:96 * r + 80, w] + d[64 * r:64 * r + 64]).astype(bf16)


def conform(lens, recv, wp, pb, gain, up, taps, dbias, down):
    bf16, f32 = jnp.bfloat16, jnp.float32
    vm = pl.BlockSpec(memory_space=pltpu.VMEM)
    return pl.pallas_call(
        conformer_kernel,
        out_shape=jax.ShapeDtypeStruct((4, 64, 1024), bf16),
        in_specs=[pl.BlockSpec(memory_space=pltpu.SMEM)] + [vm] * 8,
        out_specs=vm,
        scratch_shapes=[
            pltpu.VMEM((512, 512), bf16),
            pltpu.VMEM((512, 1024), f32),
            pltpu.VMEM((384, 1024), f32),
            pltpu.VMEM((512, 1024), bf16),
            pltpu.VMEM((512, 256), f32),
            pltpu.VMEM((512, 256), f32),
            pltpu.VMEM((8, 4, 128, 128), f32),
            pltpu.VMEM((384, 1024), bf16),
        ],
        compiler_params=pltpu.CompilerParams(vmem_limit_bytes=40 << 20),
        name="conform",
    )(lens, recv, wp, pb, gain, up, taps, dbias, down)


def per_device(waveforms, utt_len, pack_order, conv_first, conv_mid, conv_last, conv_bias, conv_gain,
               conv_shift, proj_gain, proj_shift, proj_weight, proj_bias, conf_gain, conf_up,
               conf_depth, depth_bias, conf_down):
    utts = exchange_audio(waveforms)
    frames = encode(utt_len, pack_order, utts, *prepare(conv_first, conv_mid, conv_last, conv_bias),
                    conv_gain, conv_shift, proj_gain[None], proj_shift[None])
    recv = exchange_frames(frames)
    return conform(utt_len, recv, proj_weight, proj_bias[None], conf_gain, conf_up, conf_depth,
                   depth_bias, conf_down)


def solution(mesh):
    return jax.shard_map(
        per_device,
        mesh=mesh,
        in_specs=(P(("dp", "seq"), None), P("dp", None), P("dp", None)) + (P(),) * 15,
        out_specs=P("dp", "seq", None),
        check_vma=False,
    )
```

```python
import jax
import jax.numpy as jnp
from jax import lax
from jax.experimental import pallas as pl
from jax.experimental.pallas import tpu as pltpu
from jax.sharding import PartitionSpec as P

EPS = 1e-05
QH = tuple(2.0 * c * 4.0 ** i for i, c in enumerate((0.7976911, 0.03672923, -0.00025450048, -8.666277e-06)))
MESH = pl.DeviceIdType.MESH
VM = pl.BlockSpec(memory_space=pltpu.VMEM)
SM = pl.BlockSpec(memory_space=pltpu.SMEM)
ANY = pl.BlockSpec(memory_space=pl.ANY)


def audio_kernel(waves, first, mid, last, bias_in, out, weights, taps, bias,
                 stage, held, w, t32, t16, ssem, rsem, wsem, osem):
    f32, bf16 = jnp.float32, jnp.bfloat16
    dp, seq = lax.axis_index("dp"), lax.axis_index("seq")
    mine = seq == dp // 2
    barrier = pltpu.get_barrier_semaphore()

    def source(k):
        return {"dp": 4 * (seq // 2) + k, "seq": dp // 2}

    for k in range(4):
        @pl.when(jnp.logical_not(jnp.logical_and(mine, dp % 4 == k)))
        def _():
            pl.semaphore_signal(barrier, inc=1, device_id=source(k), device_id_type=MESH)

    def fetch(b):
        src = mid.at[pl.ds(1024 * b, 1024)] if b < 6 else last.at[pl.ds(1024 * (b - 6), 1024)]
        return pltpu.make_async_copy(src, w.at[pl.ds(1024 * b, 1024)], wsem.at[b])

    def leave(b):
        at = pl.ds(1024 * b, 1024)
        return pltpu.make_async_copy(w.at[at], weights.at[at], osem.at[b])

    for b in range(8):
        fetch(b).start()

    def unfold(i, _):
        for e in range(2):
            stage[e, pl.ds(i, 1), :] = waves[e:e + 1, pl.ds(pl.multiple_of(128 * i, 128), 128)]
        return 0
    lax.fori_loop(0, 320, unfold, 0, unroll=8)
    held[...] = stage[...].astype(bf16)
    pl.semaphore_wait(barrier, jnp.where(mine, 3, 4))
    slot = dp % 4

    def copy(e, c):
        return pltpu.make_async_remote_copy(
            src_ref=held.at[e], dst_ref=out.at[slot],
            send_sem=ssem.at[2 * e + c], recv_sem=rsem.at[slot],
            device_id={"dp": 2 * seq + e, "seq": 2 * (dp // 4) + c}, device_id_type=MESH)

    def here(e, c):
        return jnp.logical_and(mine, jnp.logical_and(dp % 2 == e, seq % 2 == c))

    def local(e, c):
        return pltpu.make_async_copy(held.at[e], out.at[slot], ssem.at[2 * e + c])

    for e in range(2):
        for c in range(2):
            @pl.when(jnp.logical_not(here(e, c)))
            def _():
                copy(e, c).start()

            @pl.when(here(e, c))
            def _():
                local(e, c).start()

    b0 = bias_in[...] - jnp.mean(bias_in[...], axis=-1, keepdims=True)
    bias[...] = b0
    fw = first[...] - jnp.mean(first[...], axis=-1, keepdims=True)
    hi = b0[0:1].astype(bf16).astype(f32)
    t32[...] = jnp.zeros_like(t32)
    for v in range(8):
        t32[v, 5 * v:5 * v + 10, :] = fw
        t32[v, 126:127, :] = hi
        t32[v, 127:128, :] = b0[0:1] - hi
    t16[...] = t32[...].astype(bf16)
    pltpu.make_async_copy(t16, taps, osem.at[8]).start()
    for b in range(8):
        fetch(b).wait()

        def centre(i, _):
            at = pl.ds(pl.multiple_of(1024 * b + 16 * i, 16), 16)
            x = w[at, :].astype(f32)
            w[at, :] = (x - jnp.mean(x, axis=-1, keepdims=True)).astype(bf16)
            return 0
        lax.fori_loop(0, 64, centre, 0, unroll=4)
        leave(b).start()

    for k in range(4):
        @pl.when(jnp.logical_not(jnp.logical_and(mine, slot == k)))
        def _():
            pltpu.make_async_remote_copy(
                src_ref=held.at[0], dst_ref=out.at[k], send_sem=ssem.at[0], recv_sem=rsem.at[k],
                device_id=source(k), device_id_type=MESH).wait_recv()
    for e in range(2):
        for c in range(2):
            @pl.when(jnp.logical_not(here(e, c)))
            def _():
                copy(e, c).wait_send()

            @pl.when(here(e, c))
            def _():
                local(e, c).wait()
    pltpu.make_async_copy(t16, taps, osem.at[8]).wait()
    for b in range(8):
        leave(b).wait()


def exchange_audio(waves, first, mid, last, bias):
    bf16, f32 = jnp.bfloat16, jnp.float32
    return pl.pallas_call(
        audio_kernel,
        out_shape=(jax.ShapeDtypeStruct((4, 320, 128), bf16), jax.ShapeDtypeStruct((8192, 512), bf16),
                   jax.ShapeDtypeStruct((8, 128, 512), bf16), jax.ShapeDtypeStruct((7, 512), f32)),
        in_specs=[VM, VM, ANY, ANY, VM],
        out_specs=(ANY, ANY, ANY, VM),
        scratch_shapes=[
            pltpu.VMEM((2, 320, 128), f32),
            pltpu.VMEM((2, 320, 128), bf16),
            pltpu.VMEM((8192, 512), bf16),
            pltpu.VMEM((8, 128, 512), f32),
            pltpu.VMEM((8, 128, 512), bf16),
            pltpu.SemaphoreType.DMA((4,)),
            pltpu.SemaphoreType.DMA((4,)),
            pltpu.SemaphoreType.DMA((8,)),
            pltpu.SemaphoreType.DMA((9,)),
        ],
        compiler_params=pltpu.CompilerParams(collective_id=1, has_side_effects=True, vmem_limit_bytes=24 << 20),
        name="audio",
    )(waves, first, mid.reshape(6144, 512), last.reshape(2048, 512), bias)


def half_gelu(h):
    h = h.astype(jnp.bfloat16)
    u = jnp.minimum(h * h, jnp.bfloat16(6.25))
    q = jnp.bfloat16(QH[3])
    for c in QH[2::-1]:
        q = q * u + jnp.bfloat16(c)
    return h + h * jnp.tanh(h * q)


def finish(v, gain, shift):
    ss = jnp.sum(v * v, axis=-1, keepdims=True)
    r = lax.rsqrt(ss * (1.0 / 512) + EPS)
    return half_gelu((v * r) * gain + shift)


def encoder_kernel(lens, order, utts_in, taps_in, w_in, bias, gain, shift, pgain, pshift, out,
                   utts, taps, w, packed, lhs, y0, y1, e1, e2, e3, e4, e5, e6, halo, out32, sem):
    f32, bf16 = jnp.float32, jnp.bfloat16
    seq = lax.axis_index("seq")
    own, core = seq // 2, seq % 2
    bounds = (0, 1536, 3072, 4608, 6144, 7168, 8192)

    def fetch(k):
        if k == 0:
            return pltpu.make_async_copy(utts_in, utts, sem.at[0])
        if k == 1:
            return pltpu.make_async_copy(taps_in, taps, sem.at[1])
        at = pl.ds(bounds[k - 2], bounds[k - 1] - bounds[k - 2])
        return pltpu.make_async_copy(w_in.at[at], w.at[at], sem.at[k])

    for k in range(8):
        fetch(k).start()
    packed[...] = jnp.zeros_like(packed)
    lane = lax.broadcasted_iota(jnp.int32, (320, 128), 1)
    sample = lax.broadcasted_iota(jnp.int32, (320, 128), 0) * 128 + lane
    fetch(0).wait()
    off = jnp.int32(0)
    for p in range(4):
        u = order[own, p]
        ln = lens[own, u]
        a, b = off // 128, off % 128
        part = jnp.where(sample < ln, utts[u].astype(f32), 0.0)
        rolled = pltpu.roll(part, b, 1)
        packed[pl.ds(a, 320), :] += jnp.where(lane >= b, rolled, 0.0)
        packed[pl.ds(a + 1, 320), :] += jnp.where(lane < b, rolled, 0.0)
        off = off + ln
    nv = ((off + 10239) // 10240 - core + 1) // 2

    def row(ref, l):
        return ref[pl.ds(l, 1), :]

    def dot_(a, b):
        return jnp.dot(a, b, preferred_element_type=f32)

    def epi(y, l, groups, dst):
        g, s = row(gain, l) * 0.5, row(shift, l) * 0.5
        b = row(bias, l)
        for k in range(groups):
            v = y[pl.ds(16 * k, 16), :]
            if l > 0:
                v = v + b
            dst(k, finish(v, g, s))

    def conv3(src, l, start, rows, gap, y):
        at = 1536 * l
        y[pl.ds(0, rows), :] = dot_(src[pl.ds(start, rows), :], w[at:at + 1024, :]) + dot_(
            src[pl.ds(start + gap, rows), 0:512], w[at + 1024:at + 1536, :])

    def put(ref, gap, base=0):
        def at(k, v):
            ref[pl.ds((k // 2) * gap + base, 16), (k % 2) * 512:(k % 2) * 512 + 512] = v
        return at

    lane16 = lax.broadcasted_iota(jnp.int32, (16, 128), 1)
    row16 = lax.broadcasted_iota(jnp.int32, (16, 512), 0)

    def windows(cols, count):
        for q in range(count):
            j, o = divmod(40 * q, 128)
            x = cols[j] if o == 0 else pltpu.roll(cols[j], 128 - o, 1)
            if o + 45 > 128:
                x = jnp.where(lane16 < 128 - o, x, pltpu.roll(cols[j + 1], 128 - o, 1))
            x = jnp.where(lane16 >= 126, 1.0, x)
            lhs[pl.ds(16 * q, 16), :] = x.astype(bf16)

    after = packed[pl.ds(80 * core + 80, 8, stride=160), :]
    windows([jnp.concatenate([after, jnp.zeros((8, 128), f32)], axis=0)], 2)
    fetch(1).wait()
    for v in range(8):
        y0[pl.ds(32 * v, 32), :] = dot_(lhs[0:32, :], taps[v])

    def put_first(k, val):
        ph = 8 * (k % 2) + k // 2
        e1[pl.ds(16 * (ph // 2), 16), (ph % 2) * 512:(ph % 2) * 512 + 512] = val
    epi(y0, 0, 16, put_first)
    fetch(2).wait()
    conv3(e1, 0, 0, 112, 16, y0)
    epi(y0, 1, 7, put(e2, 16))
    fetch(3).wait()
    conv3(e2, 1, 0, 48, 16, y0)
    epi(y0, 2, 3, put(e3, 16))
    fetch(4).wait()
    conv3(e3, 2, 0, 16, 16, y0)

    def keep4(k, val):
        halo[48:64, :] = val.astype(f32)
    epi(y0, 3, 1, keep4)
    for k, e in enumerate((e1, e2, e3)):
        halo[16 * k:16 * k + 16, :] = e[0:16, 0:512].astype(f32)
    silent = jnp.broadcast_to(halo[56:57, :], (16, 512)).astype(bf16)

    def fill(i, _):
        for k in range(17):
            e4[pl.ds((k // 2) * 128 + 16 * i, 16), (k % 2) * 512:(k % 2) * 512 + 512] = silent
        return 0
    lax.fori_loop(nv, 8, fill, 0)

    def wrap(e, l, i, first, last):
        x = pltpu.roll(e[pl.ds(first, 16), 0:512].astype(f32), 15, 0)
        x = jnp.where(row16 == 15, halo[pl.ds(16 * l + i, 1), :], x)
        e[pl.ds(last, 16), 0:512] = x.astype(bf16)

    def segment(i, _):
        base = 5 * (32 * i + 16 * core)
        windows([packed[pl.ds(base + j, 16, stride=5), :] for j in range(6)], 16)

        def first(v, y):
            y[...] = dot_(lhs[...], taps[v])

        def put1(v):
            def at(q, val):
                e1[pl.ds(64 * q + 16 * (v // 2), 16), 512 * (v % 2):512 * (v % 2) + 512] = val
            return at
        ys = (y0, y1)
        first(0, y0)
        for v in range(8):
            if v < 7:
                first(v + 1, ys[(v + 1) % 2])
            epi(ys[v % 2], 0, 16, put1(v))
        wrap(e1, 0, i, 0, 1024)
        conv3(e1, 0, 0, 256, 16, y0)
        conv3(e1, 0, 256, 256, 16, y1)
        epi(y0, 1, 16, put(e2, 16, 0))
        conv3(e1, 0, 512, 256, 16, y0)
        epi(y1, 1, 16, put(e2, 16, 128))
        conv3(e1, 0, 768, 256, 16, y1)
        epi(y0, 1, 16, put(e2, 16, 256))
        conv3(e2, 1, 0, 256, 16, y0)
        epi(y1, 1, 16, put(e2, 16, 384))
        wrap(e2, 1, i, 0, 512)
        conv3(e2, 1, 256, 256, 16, y1)
        epi(y0, 2, 16, put(e3, 16, 0))
        epi(y1, 2, 16, put(e3, 16, 128))
        wrap(e3, 2, i, 0, 256)
        conv3(e3, 2, 0, 256, 16, y0)
        at = pl.multiple_of(16 * i, 16)
        epi(y0, 3, 16, put(e4, 128, at))
        wrap(e4, 3, i, at, 1024 + at)
        return 0
    lax.fori_loop(0, nv, segment, 0)
    for k in range(5, 8):
        fetch(k).wait()

    def conv2(src, l, start, y):
        y[...] = dot_(src[pl.ds(start, 256), :], w[6144 + 1024 * l:7168 + 1024 * l, :])

    def put8(ref, base):
        def at(k, v):
            ref[pl.ds(base + 16 * (k % 8), 16), (k // 8) * 512:(k // 8) * 512 + 512] = v
        return at
    conv3(e4, 3, 0, 256, 128, y0)
    conv3(e4, 3, 256, 256, 128, y1)
    epi(y0, 4, 16, put8(e5, 0))
    conv3(e4, 3, 512, 256, 128, y0)
    epi(y1, 4, 16, put8(e5, 128))
    conv3(e4, 3, 768, 256, 128, y1)
    epi(y0, 4, 16, put8(e5, 256))
    conv2(e5, 0, 0, y0)
    epi(y1, 4, 16, put8(e5, 384))
    conv2(e5, 0, 256, y1)
    epi(y0, 5, 16, put8(e6, 0))
    epi(y1, 5, 16, put8(e6, 128))
    conv2(e6, 1, 0, y0)
    pg, ps = pgain[...], pshift[...]

    def last(k, v):
        v = v.astype(f32)
        v = v - jnp.mean(v, axis=-1, keepdims=True)
        v = v * lax.rsqrt(jnp.mean(v * v, axis=-1, keepdims=True) + EPS) * pg + ps
        for c in range(4):
            out32[c, pl.ds(32 * (k % 8) + k // 8, 16, stride=2), :] = v[:, 128 * c:128 * c + 128]
    epi(y0, 6, 16, last)
    out[0:32, :] = jnp.zeros((32, 512), bf16)
    out[288:320, :] = jnp.zeros((32, 512), bf16)
    for c in range(4):
        out[32:288, 128 * c:128 * c + 128] = out32[c].astype(bf16)


def encode(lens, order, utts, taps, weights, bias, gain, shift, pgain, pshift):
    bf16, f32 = jnp.bfloat16, jnp.float32
    return pl.pallas_call(
        encoder_kernel,
        out_shape=jax.ShapeDtypeStruct((320, 512), bf16),
        in_specs=[SM, SM, ANY, ANY, ANY] + [VM] * 5,
        out_specs=VM,
        scratch_shapes=[
            pltpu.VMEM((4, 320, 128), bf16),
            pltpu.VMEM((8, 128, 512), bf16),
            pltpu.VMEM((8192, 512), bf16),
            pltpu.VMEM((1296, 128), f32),
            pltpu.VMEM((256, 128), bf16),
            pltpu.VMEM((256, 512), f32),
            pltpu.VMEM((256, 512), f32),
            pltpu.VMEM((65 * 16, 1024), bf16),
            pltpu.VMEM((33 * 16, 1024), bf16),
            pltpu.VMEM((17 * 16, 1024), bf16),
            pltpu.VMEM((9 * 128, 1024), bf16),
            pltpu.VMEM((4 * 128, 1024), bf16),
            pltpu.VMEM((2 * 128, 1024), bf16),
            pltpu.VMEM((64, 512), f32),
            pltpu.VMEM((4, 256, 128), f32),
            pltpu.SemaphoreType.DMA((8,)),
        ],
        compiler_params=pltpu.CompilerParams(vmem_limit_bytes=40 << 20),
        name="encode",
    )(lens, order, utts, taps, weights, bias, gain, shift, pgain, pshift)


def frames_kernel(frames, out, ssem, rsem):
    seq = lax.axis_index("seq")
    barrier = pltpu.get_barrier_semaphore()
    for o in range(1, 8):
        pl.semaphore_signal(barrier, inc=1, device_id={"seq": (seq + o) % 8}, device_id_type=MESH)

    def piece(d):
        return frames.at[pl.ds(pl.multiple_of(32 * d + 32 * (1 - seq % 2), 32), 64)]

    def copy(o):
        d = (seq + o) % 8
        return pltpu.make_async_remote_copy(
            src_ref=piece(d), dst_ref=out.at[seq], send_sem=ssem.at[o], recv_sem=rsem.at[seq],
            device_id={"seq": d}, device_id_type=MESH)
    own = pltpu.make_async_copy(piece(seq), out.at[seq], ssem.at[0])
    own.start()
    pl.semaphore_wait(barrier, 7)
    for o in range(1, 8):
        copy(o).start()
    own.wait()
    for o in range(1, 8):
        d = (seq + o) % 8
        pltpu.make_async_remote_copy(
            src_ref=piece(d), dst_ref=out.at[d], send_sem=ssem.at[o], recv_sem=rsem.at[d],
            device_id={"seq": d}, device_id_type=MESH).wait_recv()
    for o in range(1, 8):
        copy(o).wait_send()


def exchange_frames(frames):
    return pl.pallas_call(
        frames_kernel,
        out_shape=jax.ShapeDtypeStruct((8, 64, 512), jnp.bfloat16),
        in_specs=[ANY],
        out_specs=ANY,
        scratch_shapes=[pltpu.SemaphoreType.DMA((8,)), pltpu.SemaphoreType.DMA((8,))],
        compiler_params=pltpu.CompilerParams(collective_id=2, has_side_effects=True, vmem_limit_bytes=1 << 20),
        name="frames",
    )(frames)


def conformer_kernel(lens, recv_in, wp_in, pb, gain, up_in, taps, dbias, down_in, out,
                     recv, wp, up, down, nrm, s0, s1, lifted, ya, yb, g, act, sem):
    f32, bf16 = jnp.float32, jnp.bfloat16
    pairs = ((recv_in, recv), (wp_in, wp), (up_in.at[0], up.at[0]), (down_in.at[0], down.at[0]),
             (up_in.at[1], up.at[1]), (down_in.at[1], down.at[1]))

    def fetch(k):
        return pltpu.make_async_copy(pairs[k][0], pairs[k][1], sem.at[k])
    for k in range(6):
        fetch(k).start()
    fetch(0).wait()
    base = 64 * lax.axis_index("seq") - 32
    for r in range(4):
        for c in range(4):
            nrm[128 * r + 32 * c:128 * r + 32 * c + 32, :] = recv[2 * r + (c + 1) % 2, 32 * (c // 2):32 * (c // 2) + 32, :]

    def dot_(a, b):
        return jnp.dot(a, b, preferred_element_type=f32)

    fetch(1).wait()
    for n in range(4):
        w = slice(256 * n, 256 * n + 256)
        s0[:, w] = dot_(nrm[...], wp[:, w]) + pb[:, w]

    def norm(src, l, rows):
        gl = gain[l:l + 1, :]

        def body(i, _):
            at = pl.ds(pl.multiple_of(16 * i, 16), 16)
            v = src[at, :]
            v = v - jnp.mean(v, axis=-1, keepdims=True)
            v = v * lax.rsqrt(jnp.mean(v * v, axis=-1, keepdims=True) + EPS) * gl
            lifted[at, :] = v.astype(bf16)
            return 0
        lax.fori_loop(0, rows // 16, body, 0, unroll=2)

    def module(l, per, lo, keep):
        rows = 4 * per

        def chunk(n, _):
            wa = pl.ds(pl.multiple_of(256 * n, 256), 256)
            wb = pl.ds(pl.multiple_of(1024 + 256 * n, 256), 256)
            ya[0:rows, :] = dot_(lifted[0:rows, :], up[l, :, wa])
            yb[0:rows, :] = dot_(lifted[0:rows, :], up[l, :, wb])
            for r in range(4):
                total = lens[r, 0] + lens[r, 1] + lens[r, 2] + lens[r, 3]
                valid = (total - 400) // 320 + 1
                for k in range(per // 16):
                    at = slice(per * r + 16 * k, per * r + 16 * k + 16)
                    t = base + lo + 16 * k + lax.broadcasted_iota(jnp.int32, (16, 256), 0)
                    live = jnp.logical_and(t >= 0, t < valid)
                    v = jnp.where(live, ya[at, :] * jax.nn.sigmoid(yb[at, :]), 0.0)
                    g[2 * n, r, lo + 16 * k:lo + 16 * k + 16, :] = v[:, 0:128]
                    g[2 * n + 1, r, lo + 16 * k:lo + 16 * k + 16, :] = v[:, 128:256]
            return 0
        lax.fori_loop(0, 4, chunk, 0)
        first = 64 - keep // 2

        def depth(c, _):
            w = pl.ds(pl.multiple_of(128 * c, 128), 128)

            def one(r, _):
                acc = jnp.broadcast_to(dbias[l:l + 1, w], (keep, 128))
                for j in range(31):
                    acc = acc + g[c, r, first + j - 15:first + j - 15 + keep, :] * taps[j, l:l + 1, w]
                act[pl.ds(pl.multiple_of(keep * r, 32), keep), w] = (acc * jax.nn.sigmoid(acc)).astype(bf16)
                return 0
            return lax.fori_loop(0, 4, one, 0)
        lax.fori_loop(0, 8, depth, 0)

    norm(s0, 0, 512)
    fetch(2).wait()
    module(0, 128, 0, 96)
    fetch(3).wait()
    for n in range(4):
        w = slice(256 * n, 256 * n + 256)
        d = dot_(act[...], down[0, :, w])
        for r in range(4):
            s1[96 * r:96 * r + 96, w] = s0[128 * r + 16:128 * r + 112, w] + d[96 * r:96 * r + 96]
    norm(s1, 1, 384)
    fetch(4).wait()
    module(1, 96, 16, 64)
    fetch(5).wait()
    for n in range(4):
        w = slice(256 * n, 256 * n + 256)
        d = dot_(act[0:256, :], down[1, :, w])
        for r in range(4):
            out[r, :, w] = (s1[96 * r + 16:96 * r + 80, w] + d[64 * r:64 * r + 64]).astype(bf16)


def conform(lens, recv, wp, pb, gain, up, taps, dbias, down):
    bf16, f32 = jnp.bfloat16, jnp.float32
    return pl.pallas_call(
        conformer_kernel,
        out_shape=jax.ShapeDtypeStruct((4, 64, 1024), bf16),
        in_specs=[SM, ANY, ANY, VM, VM, ANY, VM, VM, ANY],
        out_specs=VM,
        scratch_shapes=[
            pltpu.VMEM((8, 64, 512), bf16),
            pltpu.VMEM((512, 1024), bf16),
            pltpu.VMEM((2, 1024, 2048), bf16),
            pltpu.VMEM((2, 1024, 1024), bf16),
            pltpu.VMEM((512, 512), bf16),
            pltpu.VMEM((512, 1024), f32),
            pltpu.VMEM((384, 1024), f32),
            pltpu.VMEM((512, 1024), bf16),
            pltpu.VMEM((512, 256), f32),
            pltpu.VMEM((512, 256), f32),
            pltpu.VMEM((8, 4, 128, 128), f32),
            pltpu.VMEM((384, 1024), bf16),
            pltpu.SemaphoreType.DMA((6,)),
        ],
        compiler_params=pltpu.CompilerParams(vmem_limit_bytes=40 << 20),
        name="conform",
    )(lens, recv, wp, pb, gain, up, jnp.transpose(taps, (1, 0, 2)), dbias, down)


def per_device(waveforms, utt_len, pack_order, conv_first, conv_mid, conv_last, conv_bias, conv_gain,
               conv_shift, proj_gain, proj_shift, proj_weight, proj_bias, conf_gain, conf_up,
               conf_depth, depth_bias, conf_down):
    utts, weights, taps, bias = exchange_audio(waveforms, conv_first, conv_mid, conv_last, conv_bias)
    frames = encode(utt_len, pack_order, utts, taps, weights, bias, conv_gain, conv_shift,
                    proj_gain[None], proj_shift[None])
    recv = exchange_frames(frames)
    return conform(utt_len, recv, proj_weight, proj_bias[None], conf_gain, conf_up, conf_depth,
                   depth_bias, conf_down)


def solution(mesh):
    return jax.shard_map(
        per_device,
        mesh=mesh,
        in_specs=(P(("dp", "seq"), None), P("dp", None), P("dp", None)) + (P(),) * 15,
        out_specs=P("dp", "seq", None),
        check_vma=False,
    )
```

```python
import jax
import jax.numpy as jnp
from jax import lax
from jax.experimental import pallas as pl
from jax.experimental.pallas import tpu as pltpu
from jax.sharding import PartitionSpec as P

EPS = 1e-05
QH = tuple(2.0 * c * 4.0 ** i for i, c in enumerate((0.7976911, 0.03672923, -0.00025450048, -8.666277e-06)))
MESH = pl.DeviceIdType.MESH
VM = pl.BlockSpec(memory_space=pltpu.VMEM)
SM = pl.BlockSpec(memory_space=pltpu.SMEM)
ANY = pl.BlockSpec(memory_space=pl.ANY)
HBM = pl.BlockSpec(memory_space=pltpu.HBM)


def audio_kernel(waves_in, first_in, mid, last, bias_in, out, weights, taps, bias,
                 waves, first, bias_raw, stage, held, raw, w, means, t32, t16, ssem, rsem, wsem, osem):
    f32, bf16 = jnp.float32, jnp.bfloat16
    dp, seq = lax.axis_index("dp"), lax.axis_index("seq")
    mine = seq == dp // 2
    barrier = pltpu.get_barrier_semaphore()

    def source(k):
        return {"dp": 4 * (seq // 2) + k, "seq": dp // 2}

    for k in range(4):
        @pl.when(jnp.logical_not(jnp.logical_and(mine, dp % 4 == k)))
        def _():
            pl.semaphore_signal(barrier, inc=1, device_id=source(k), device_id_type=MESH)

    def fetch(b):
        src = mid.at[pl.ds(1024 * b, 1024)] if b < 6 else last.at[pl.ds(1024 * (b - 6), 1024)]
        return pltpu.make_async_copy(src, raw.at[pl.ds(1024 * b, 1024)], wsem.at[b])

    def leave(b):
        at = pl.ds(1024 * b, 1024)
        return pltpu.make_async_copy(w.at[at], weights.at[at], osem.at[b])

    small = [pltpu.make_async_copy(x, y, wsem.at[8 + k]) for k, (x, y) in enumerate(
        ((waves_in, waves), (first_in, first), (bias_in, bias_raw)))]
    for c in small:
        c.start()
    for b in range(8):
        fetch(b).start()
    small[0].wait()

    def unfold(i, _):
        for e in range(2):
            stage[e, pl.ds(i, 1), :] = waves[e:e + 1, pl.ds(pl.multiple_of(128 * i, 128), 128)]
        return 0
    lax.fori_loop(0, 320, unfold, 0, unroll=8)
    held[...] = stage[...].astype(bf16)
    pl.semaphore_wait(barrier, jnp.where(mine, 3, 4))
    slot = dp % 4

    def copy(e, c):
        return pltpu.make_async_remote_copy(
            src_ref=held.at[e], dst_ref=out.at[slot],
            send_sem=ssem.at[2 * e + c], recv_sem=rsem.at[slot],
            device_id={"dp": 2 * seq + e, "seq": 2 * (dp // 4) + c}, device_id_type=MESH)

    def here(e, c):
        return jnp.logical_and(mine, jnp.logical_and(dp % 2 == e, seq % 2 == c))

    def local(e, c):
        return pltpu.make_async_copy(held.at[e], out.at[slot], ssem.at[2 * e + c])

    for e in range(2):
        for c in range(2):
            @pl.when(jnp.logical_not(here(e, c)))
            def _():
                copy(e, c).start()

            @pl.when(here(e, c))
            def _():
                local(e, c).start()

    small[1].wait()
    small[2].wait()
    b0 = bias_raw[...] - jnp.mean(bias_raw[...], axis=-1, keepdims=True)
    bias[...] = b0
    fw = first[...] - jnp.mean(first[...], axis=-1, keepdims=True)
    hi = b0[0:1].astype(bf16).astype(f32)
    t32[...] = jnp.zeros_like(t32)
    for v in range(8):
        t32[v, 5 * v:5 * v + 10, :] = fw
        t32[v, 126:127, :] = hi
        t32[v, 127:128, :] = b0[0:1] - hi
    t16[...] = t32[...].astype(bf16)
    pltpu.make_async_copy(t16, taps, osem.at[8]).start()
    ones = jnp.full((512, 128), 1.0 / 512, bf16)
    for b in range(8):
        fetch(b).wait()
        means[...] = jnp.dot(raw[1024 * b:1024 * b + 1024, :], ones, preferred_element_type=f32)

        def centre(i, _):
            at = pl.ds(pl.multiple_of(1024 * b + 32 * i, 32), 32)
            m = means[pl.ds(pl.multiple_of(32 * i, 32), 32), :]
            for c in range(4):
                k = slice(128 * c, 128 * c + 128)
                w[at, k] = (raw[at, k].astype(f32) - m).astype(bf16)
            return 0
        lax.fori_loop(0, 32, centre, 0, unroll=4)
        leave(b).start()

    for k in range(4):
        @pl.when(jnp.logical_not(jnp.logical_and(mine, slot == k)))
        def _():
            pltpu.make_async_remote_copy(
                src_ref=held.at[0], dst_ref=out.at[k], send_sem=ssem.at[0], recv_sem=rsem.at[k],
                device_id=source(k), device_id_type=MESH).wait_recv()
    for e in range(2):
        for c in range(2):
            @pl.when(jnp.logical_not(here(e, c)))
            def _():
                copy(e, c).wait_send()

            @pl.when(here(e, c))
            def _():
                local(e, c).wait()
    pltpu.make_async_copy(t16, taps, osem.at[8]).wait()
    for b in range(8):
        leave(b).wait()


def exchange_audio(waves, first, mid, last, bias):
    bf16, f32 = jnp.bfloat16, jnp.float32
    return pl.pallas_call(
        audio_kernel,
        out_shape=(jax.ShapeDtypeStruct((4, 320, 128), bf16), jax.ShapeDtypeStruct((8192, 512), bf16),
                   jax.ShapeDtypeStruct((8, 128, 512), bf16), jax.ShapeDtypeStruct((7, 512), f32)),
        in_specs=[HBM, HBM, HBM, HBM, HBM],
        out_specs=(HBM, HBM, HBM, VM),
        scratch_shapes=[
            pltpu.VMEM((2, 40960), f32),
            pltpu.VMEM((10, 512), f32),
            pltpu.VMEM((7, 512), f32),
            pltpu.VMEM((2, 320, 128), f32),
            pltpu.VMEM((2, 320, 128), bf16),
            pltpu.VMEM((8192, 512), bf16),
            pltpu.VMEM((8192, 512), bf16),
            pltpu.VMEM((1024, 128), f32),
            pltpu.VMEM((8, 128, 512), f32),
            pltpu.VMEM((8, 128, 512), bf16),
            pltpu.SemaphoreType.DMA((4,)),
            pltpu.SemaphoreType.DMA((4,)),
            pltpu.SemaphoreType.DMA((11,)),
            pltpu.SemaphoreType.DMA((9,)),
        ],
        compiler_params=pltpu.CompilerParams(collective_id=1, has_side_effects=True, vmem_limit_bytes=26 << 20),
        name="audio",
    )(*[pltpu.with_memory_space_constraint(x, pltpu.HBM) for x in (
        waves, first, mid.reshape(6144, 512), last.reshape(2048, 512), bias)])


def half_gelu(h):
    h = h.astype(jnp.bfloat16)
    u = jnp.minimum(h * h, jnp.bfloat16(6.25))
    q = jnp.bfloat16(QH[3])
    for c in QH[2::-1]:
        q = q * u + jnp.bfloat16(c)
    return h + h * jnp.tanh(h * q)


def finish(v, gain, shift):
    ss = jnp.sum(v * v, axis=-1, keepdims=True)
    r = lax.rsqrt(ss * (1.0 / 512) + EPS)
    return half_gelu((v * r) * gain + shift)


def encoder_kernel(lens, order, utts_in, taps_in, w_in, bias, gain, shift, pgain, pshift, out,
                   utts, taps, w, packed, lhs, y0, y1, e1, e2, e3, e4, e5, e6, halo, out32, sem):
    f32, bf16 = jnp.float32, jnp.bfloat16
    seq = lax.axis_index("seq")
    own, core = seq // 2, seq % 2
    bounds = (0, 1536, 3072, 4608, 6144, 7168, 8192)

    def fetch(k):
        if k == 0:
            return pltpu.make_async_copy(utts_in, utts, sem.at[0])
        if k == 1:
            return pltpu.make_async_copy(taps_in, taps, sem.at[1])
        at = pl.ds(bounds[k - 2], bounds[k - 1] - bounds[k - 2])
        return pltpu.make_async_copy(w_in.at[at], w.at[at], sem.at[k])

    for k in range(8):
        fetch(k).start()
    packed[...] = jnp.zeros_like(packed)
    lane = lax.broadcasted_iota(jnp.int32, (320, 128), 1)
    sample = lax.broadcasted_iota(jnp.int32, (320, 128), 0) * 128 + lane
    fetch(0).wait()
    off = jnp.int32(0)
    for p in range(4):
        u = order[own, p]
        ln = lens[own, u]
        a, b = off // 128, off % 128
        part = jnp.where(sample < ln, utts[u].astype(f32), 0.0)
        rolled = pltpu.roll(part, b, 1)
        packed[pl.ds(a, 320), :] += jnp.where(lane >= b, rolled, 0.0)
        packed[pl.ds(a + 1, 320), :] += jnp.where(lane < b, rolled, 0.0)
        off = off + ln
    nv = ((off + 10239) // 10240 - core + 1) // 2

    def row(ref, l):
        return ref[pl.ds(l, 1), :]

    def dot_(a, b):
        return jnp.dot(a, b, preferred_element_type=f32)

    def epi(y, l, groups, dst):
        g, s = row(gain, l) * 0.5, row(shift, l) * 0.5
        b = row(bias, l)
        for k in range(groups):
            v = y[pl.ds(16 * k, 16), :]
            if l > 0:
                v = v + b
            dst(k, finish(v, g, s))

    def conv3(src, l, start, rows, gap, y):
        at = 1536 * l
        y[pl.ds(0, rows), :] = dot_(src[pl.ds(start, rows), :], w[at:at + 1024, :]) + dot_(
            src[pl.ds(start + gap, rows), 0:512], w[at + 1024:at + 1536, :])

    def put(ref, gap, base=0):
        def at(k, v):
            ref[pl.ds((k // 2) * gap + base, 16), (k % 2) * 512:(k % 2) * 512 + 512] = v
        return at

    lane16 = lax.broadcasted_iota(jnp.int32, (16, 128), 1)
    row16 = lax.broadcasted_iota(jnp.int32, (16, 512), 0)

    def windows(cols, count):
        for q in range(count):
            j, o = divmod(40 * q, 128)
            x = cols[j] if o == 0 else pltpu.roll(cols[j], 128 - o, 1)
            if o + 45 > 128:
                x = jnp.where(lane16 < 128 - o, x, pltpu.roll(cols[j + 1], 128 - o, 1))
            x = jnp.where(lane16 >= 126, 1.0, x)
            lhs[pl.ds(16 * q, 16), :] = x.astype(bf16)

    after = packed[pl.ds(80 * core + 80, 8, stride=160), :]
    windows([jnp.concatenate([after, jnp.zeros((8, 128), f32)], axis=0)], 2)
    fetch(1).wait()
    for v in range(8):
        y0[pl.ds(32 * v, 32), :] = dot_(lhs[0:32, :], taps[v])

    def put_first(k, val):
        ph = 8 * (k % 2) + k // 2
        e1[pl.ds(16 * (ph // 2), 16), (ph % 2) * 512:(ph % 2) * 512 + 512] = val
    epi(y0, 0, 16, put_first)
    fetch(2).wait()
    conv3(e1, 0, 0, 112, 16, y0)
    epi(y0, 1, 7, put(e2, 16))
    fetch(3).wait()
    conv3(e2, 1, 0, 48, 16, y0)
    epi(y0, 2, 3, put(e3, 16))
    fetch(4).wait()
    conv3(e3, 2, 0, 16, 16, y0)

    def keep4(k, val):
        halo[48:64, :] = val.astype(f32)
    epi(y0, 3, 1, keep4)
    for k, e in enumerate((e1, e2, e3)):
        halo[16 * k:16 * k + 16, :] = e[0:16, 0:512].astype(f32)
    silent = jnp.broadcast_to(halo[56:57, :], (16, 512)).astype(bf16)

    def fill(i, _):
        for k in range(17):
            e4[pl.ds((k // 2) * 128 + 16 * i, 16), (k % 2) * 512:(k % 2) * 512 + 512] = silent
        return 0
    lax.fori_loop(nv, 8, fill, 0)

    def wrap(e, l, i, first, last):
        x = pltpu.roll(e[pl.ds(first, 16), 0:512].astype(f32), 15, 0)
        x = jnp.where(row16 == 15, halo[pl.ds(16 * l + i, 1), :], x)
        e[pl.ds(last, 16), 0:512] = x.astype(bf16)

    def segment(i, _):
        base = 5 * (32 * i + 16 * core)
        windows([packed[pl.ds(base + j, 16, stride=5), :] for j in range(6)], 16)

        def first(v, y):
            y[...] = dot_(lhs[...], taps[v])

        def put1(v):
            def at(q, val):
                e1[pl.ds(64 * q + 16 * (v // 2), 16), 512 * (v % 2):512 * (v % 2) + 512] = val
            return at
        ys = (y0, y1)
        first(0, y0)
        for v in range(8):
            if v < 7:
                first(v + 1, ys[(v + 1) % 2])
            epi(ys[v % 2], 0, 16, put1(v))
        wrap(e1, 0, i, 0, 1024)
        conv3(e1, 0, 0, 256, 16, y0)
        conv3(e1, 0, 256, 256, 16, y1)
        epi(y0, 1, 16, put(e2, 16, 0))
        conv3(e1, 0, 512, 256, 16, y0)
        epi(y1, 1, 16, put(e2, 16, 128))
        conv3(e1, 0, 768, 256, 16, y1)
        epi(y0, 1, 16, put(e2, 16, 256))
        conv3(e2, 1, 0, 256, 16, y0)
        epi(y1, 1, 16, put(e2, 16, 384))
        wrap(e2, 1, i, 0, 512)
        conv3(e2, 1, 256, 256, 16, y1)
        epi(y0, 2, 16, put(e3, 16, 0))
        epi(y1, 2, 16, put(e3, 16, 128))
        wrap(e3, 2, i, 0, 256)
        conv3(e3, 2, 0, 256, 16, y0)
        at = pl.multiple_of(16 * i, 16)
        epi(y0, 3, 16, put(e4, 128, at))
        wrap(e4, 3, i, at, 1024 + at)
        return 0
    lax.fori_loop(0, nv, segment, 0)
    for k in range(5, 8):
        fetch(k).wait()

    def conv2(src, l, start, y):
        y[...] = dot_(src[pl.ds(start, 256), :], w[6144 + 1024 * l:7168 + 1024 * l, :])

    def put8(ref, base):
        def at(k, v):
            ref[pl.ds(base + 16 * (k % 8), 16), (k // 8) * 512:(k // 8) * 512 + 512] = v
        return at
    conv3(e4, 3, 0, 256, 128, y0)
    conv3(e4, 3, 256, 256, 128, y1)
    epi(y0, 4, 16, put8(e5, 0))
    conv3(e4, 3, 512, 256, 128, y0)
    epi(y1, 4, 16, put8(e5, 128))
    conv3(e4, 3, 768, 256, 128, y1)
    epi(y0, 4, 16, put8(e5, 256))
    conv2(e5, 0, 0, y0)
    epi(y1, 4, 16, put8(e5, 384))
    conv2(e5, 0, 256, y1)
    epi(y0, 5, 16, put8(e6, 0))
    epi(y1, 5, 16, put8(e6, 128))
    conv2(e6, 1, 0, y0)
    pg, ps = pgain[...], pshift[...]

    def last(k, v):
        v = v.astype(f32)
        v = v - jnp.mean(v, axis=-1, keepdims=True)
        v = v * lax.rsqrt(jnp.mean(v * v, axis=-1, keepdims=True) + EPS) * pg + ps
        for c in range(4):
            out32[c, pl.ds(32 * (k % 8) + k // 8, 16, stride=2), :] = v[:, 128 * c:128 * c + 128]
    epi(y0, 6, 16, last)
    out[0:32, :] = jnp.zeros((32, 512), bf16)
    out[288:320, :] = jnp.zeros((32, 512), bf16)
    for c in range(4):
        out[32:288, 128 * c:128 * c + 128] = out32[c].astype(bf16)


def encode(lens, order, utts, taps, weights, bias, gain, shift, pgain, pshift):
    bf16, f32 = jnp.bfloat16, jnp.float32
    return pl.pallas_call(
        encoder_kernel,
        out_shape=jax.ShapeDtypeStruct((320, 512), bf16),
        in_specs=[SM, SM, HBM, HBM, HBM] + [VM] * 5,
        out_specs=VM,
        scratch_shapes=[
            pltpu.VMEM((4, 320, 128), bf16),
            pltpu.VMEM((8, 128, 512), bf16),
            pltpu.VMEM((8192, 512), bf16),
            pltpu.VMEM((1296, 128), f32),
            pltpu.VMEM((256, 128), bf16),
            pltpu.VMEM((256, 512), f32),
            pltpu.VMEM((256, 512), f32),
            pltpu.VMEM((65 * 16, 1024), bf16),
            pltpu.VMEM((33 * 16, 1024), bf16),
            pltpu.VMEM((17 * 16, 1024), bf16),
            pltpu.VMEM((9 * 128, 1024), bf16),
            pltpu.VMEM((4 * 128, 1024), bf16),
            pltpu.VMEM((2 * 128, 1024), bf16),
            pltpu.VMEM((64, 512), f32),
            pltpu.VMEM((4, 256, 128), f32),
            pltpu.SemaphoreType.DMA((8,)),
        ],
        compiler_params=pltpu.CompilerParams(vmem_limit_bytes=30 << 20),
        name="encode",
    )(lens, order, utts, taps, weights, bias, gain, shift, pgain, pshift)


def frames_kernel(frames, out, ssem, rsem):
    seq = lax.axis_index("seq")
    barrier = pltpu.get_barrier_semaphore()
    for o in range(1, 8):
        pl.semaphore_signal(barrier, inc=1, device_id={"seq": (seq + o) % 8}, device_id_type=MESH)

    def piece(d):
        return frames.at[pl.ds(pl.multiple_of(32 * d + 32 * (1 - seq % 2), 32), 64)]

    def copy(o):
        d = (seq + o) % 8
        return pltpu.make_async_remote_copy(
            src_ref=piece(d), dst_ref=out.at[seq], send_sem=ssem.at[o], recv_sem=rsem.at[seq],
            device_id={"seq": d}, device_id_type=MESH)
    own = pltpu.make_async_copy(piece(seq), out.at[seq], ssem.at[0])
    own.start()
    pl.semaphore_wait(barrier, 7)
    for o in range(1, 8):
        copy(o).start()
    own.wait()
    for o in range(1, 8):
        d = (seq + o) % 8
        pltpu.make_async_remote_copy(
            src_ref=piece(d), dst_ref=out.at[d], send_sem=ssem.at[o], recv_sem=rsem.at[d],
            device_id={"seq": d}, device_id_type=MESH).wait_recv()
    for o in range(1, 8):
        copy(o).wait_send()


def exchange_frames(frames):
    return pl.pallas_call(
        frames_kernel,
        out_shape=jax.ShapeDtypeStruct((8, 64, 512), jnp.bfloat16),
        in_specs=[HBM],
        out_specs=HBM,
        scratch_shapes=[pltpu.SemaphoreType.DMA((8,)), pltpu.SemaphoreType.DMA((8,))],
        compiler_params=pltpu.CompilerParams(collective_id=2, has_side_effects=True, vmem_limit_bytes=1 << 20),
        name="frames",
    )(frames)


def conformer_kernel(lens, recv, wp, pb, gain, up, taps, dbias, down, out,
                     nrm, s0, s1, lifted, ya, yb, g, act):
    f32, bf16 = jnp.float32, jnp.bfloat16
    base = 64 * lax.axis_index("seq") - 32
    for r in range(4):
        for c in range(4):
            nrm[128 * r + 32 * c:128 * r + 32 * c + 32, :] = recv[2 * r + (c + 1) % 2, 32 * (c // 2):32 * (c // 2) + 32, :]

    def dot_(a, b):
        return jnp.dot(a, b, preferred_element_type=f32)

    for n in range(4):
        w = slice(256 * n, 256 * n + 256)
        s0[:, w] = dot_(nrm[...], wp[:, w]) + pb[:, w]

    def norm(src, l, rows):
        gl = gain[l:l + 1, :]

        def body(i, _):
            at = pl.ds(pl.multiple_of(16 * i, 16), 16)
            v = src[at, :]
            v = v - jnp.mean(v, axis=-1, keepdims=True)
            v = v * lax.rsqrt(jnp.mean(v * v, axis=-1, keepdims=True) + EPS) * gl
            lifted[at, :] = v.astype(bf16)
            return 0
        lax.fori_loop(0, rows // 16, body, 0, unroll=8)

    def module(l, per, lo, keep):
        rows = 4 * per

        def chunk(n, _):
            wa = pl.ds(pl.multiple_of(256 * n, 256), 256)
            wb = pl.ds(pl.multiple_of(1024 + 256 * n, 256), 256)
            ya[0:rows, :] = dot_(lifted[0:rows, :], up[l, :, wa])
            yb[0:rows, :] = dot_(lifted[0:rows, :], up[l, :, wb])
            for r in range(4):
                total = lens[r, 0] + lens[r, 1] + lens[r, 2] + lens[r, 3]
                valid = (total - 400) // 320 + 1
                for k in range(per // 16):
                    at = slice(per * r + 16 * k, per * r + 16 * k + 16)
                    t = base + lo + 16 * k + lax.broadcasted_iota(jnp.int32, (16, 256), 0)
                    live = jnp.logical_and(t >= 0, t < valid)
                    v = jnp.where(live, ya[at, :] * jax.nn.sigmoid(yb[at, :]), 0.0)
                    g[2 * n, r, lo + 16 * k:lo + 16 * k + 16, :] = v[:, 0:128]
                    g[2 * n + 1, r, lo + 16 * k:lo + 16 * k + 16, :] = v[:, 128:256]
            return 0
        lax.fori_loop(0, 4, chunk, 0)
        first = 64 - keep // 2

        def depth(c, _):
            w = pl.ds(pl.multiple_of(128 * c, 128), 128)

            def one(r, _):
                acc = jnp.broadcast_to(dbias[l:l + 1, w], (keep, 128))
                for j in range(31):
                    acc = acc + g[c, r, first + j - 15:first + j - 15 + keep, :] * taps[j, l:l + 1, w]
                act[pl.ds(pl.multiple_of(keep * r, 32), keep), w] = (acc * jax.nn.sigmoid(acc)).astype(bf16)
                return 0
            return lax.fori_loop(0, 4, one, 0)
        lax.fori_loop(0, 8, depth, 0)

    norm(s0, 0, 512)
    module(0, 128, 0, 96)
    for n in range(4):
        w = slice(256 * n, 256 * n + 256)
        d = dot_(act[...], down[0, :, w])
        for r in range(4):
            s1[96 * r:96 * r + 96, w] = s0[128 * r + 16:128 * r + 112, w] + d[96 * r:96 * r + 96]
    norm(s1, 1, 384)
    module(1, 96, 16, 64)
    for n in range(4):
        w = slice(256 * n, 256 * n + 256)
        d = dot_(act[0:256, :], down[1, :, w])
        for r in range(4):
            out[r, :, w] = (s1[96 * r + 16:96 * r + 80, w] + d[64 * r:64 * r + 64]).astype(bf16)


def conform(lens, recv, wp, pb, gain, up, taps, dbias, down):
    bf16, f32 = jnp.bfloat16, jnp.float32
    return pl.pallas_call(
        conformer_kernel,
        out_shape=jax.ShapeDtypeStruct((4, 64, 1024), bf16),
        in_specs=[SM] + [VM] * 8,
        out_specs=VM,
        scratch_shapes=[
            pltpu.VMEM((512, 512), bf16),
            pltpu.VMEM((512, 1024), f32),
            pltpu.VMEM((384, 1024), f32),
            pltpu.VMEM((512, 1024), bf16),
            pltpu.VMEM((512, 256), f32),
            pltpu.VMEM((512, 256), f32),
            pltpu.VMEM((8, 4, 128, 128), f32),
            pltpu.VMEM((384, 1024), bf16),
        ],
        compiler_params=pltpu.CompilerParams(vmem_limit_bytes=20 << 20),
        name="conform",
    )(lens, recv, wp, pb, gain, up, jnp.transpose(taps, (1, 0, 2)), dbias, down)


def per_device(waveforms, utt_len, pack_order, conv_first, conv_mid, conv_last, conv_bias, conv_gain,
               conv_shift, proj_gain, proj_shift, proj_weight, proj_bias, conf_gain, conf_up,
               conf_depth, depth_bias, conf_down):
    utts, weights, taps, bias = exchange_audio(waveforms, conv_first, conv_mid, conv_last, conv_bias)
    frames = encode(utt_len, pack_order, utts, taps, weights, bias, conv_gain, conv_shift,
                    proj_gain[None], proj_shift[None])
    recv = exchange_frames(frames)
    return conform(utt_len, recv, proj_weight, proj_bias[None], conf_gain, conf_up, conf_depth,
                   depth_bias, conf_down)


def solution(mesh):
    return jax.shard_map(
        per_device,
        mesh=mesh,
        in_specs=(P(("dp", "seq"), None), P("dp", None), P("dp", None)) + (P(),) * 15,
        out_specs=P("dp", "seq", None),
        check_vma=False,
    )
```

```python
import jax
import jax.numpy as jnp
from jax import lax
from jax.experimental import pallas as pl
from jax.experimental.pallas import tpu as pltpu
from jax.sharding import PartitionSpec as P

EPS = 1e-05
QH = tuple(2.0 * c * 4.0 ** i for i, c in enumerate((0.7976911, 0.03672923, -0.00025450048, -8.666277e-06)))
MESH = pl.DeviceIdType.MESH
VM = pl.BlockSpec(memory_space=pltpu.VMEM)
SM = pl.BlockSpec(memory_space=pltpu.SMEM)
ANY = pl.BlockSpec(memory_space=pl.ANY)
HBM = pl.BlockSpec(memory_space=pltpu.HBM)


def audio_kernel(waves_in, first_in, mid, last, bias_in, out, weights, taps, bias,
                 waves, first, bias_raw, stage, held, raw, w, t32, t16, ssem, rsem, wsem, osem):
    f32, bf16 = jnp.float32, jnp.bfloat16
    dp, seq = lax.axis_index("dp"), lax.axis_index("seq")
    mine = seq == dp // 2
    barrier = pltpu.get_barrier_semaphore()

    def source(k):
        return {"dp": 4 * (seq // 2) + k, "seq": dp // 2}

    for k in range(4):
        @pl.when(jnp.logical_not(jnp.logical_and(mine, dp % 4 == k)))
        def _():
            pl.semaphore_signal(barrier, inc=1, device_id=source(k), device_id_type=MESH)

    def fetch(b):
        src = mid.at[pl.ds(1024 * b, 1024)] if b < 6 else last.at[pl.ds(1024 * (b - 6), 1024)]
        return pltpu.make_async_copy(src, raw.at[pl.ds(1024 * b, 1024)], wsem.at[b])

    def leave(b):
        at = pl.ds(1024 * b, 1024)
        return pltpu.make_async_copy(w.at[at], weights.at[at], osem.at[b])

    small = [pltpu.make_async_copy(x, y, wsem.at[8 + k]) for k, (x, y) in enumerate(
        ((waves_in, waves), (first_in, first), (bias_in, bias_raw)))]
    for c in small:
        c.start()
    for b in range(8):
        fetch(b).start()
    small[0].wait()

    def unfold(i, _):
        for e in range(2):
            stage[e, pl.ds(i, 1), :] = waves[e:e + 1, pl.ds(pl.multiple_of(128 * i, 128), 128)]
        return 0
    lax.fori_loop(0, 320, unfold, 0, unroll=8)
    held[...] = stage[...].astype(bf16)
    pl.semaphore_wait(barrier, jnp.where(mine, 3, 4))
    slot = dp % 4

    def copy(e, c):
        return pltpu.make_async_remote_copy(
            src_ref=held.at[e], dst_ref=out.at[slot],
            send_sem=ssem.at[2 * e + c], recv_sem=rsem.at[slot],
            device_id={"dp": 2 * seq + e, "seq": 2 * (dp // 4) + c}, device_id_type=MESH)

    def here(e, c):
        return jnp.logical_and(mine, jnp.logical_and(dp % 2 == e, seq % 2 == c))

    def local(e, c):
        return pltpu.make_async_copy(held.at[e], out.at[slot], ssem.at[2 * e + c])

    for e in range(2):
        for c in range(2):
            @pl.when(jnp.logical_not(here(e, c)))
            def _():
                copy(e, c).start()

            @pl.when(here(e, c))
            def _():
                local(e, c).start()

    small[1].wait()
    small[2].wait()
    b0 = bias_raw[...] - jnp.mean(bias_raw[...], axis=-1, keepdims=True)
    bias[...] = b0
    fw = first[...] - jnp.mean(first[...], axis=-1, keepdims=True)
    hi = b0[0:1].astype(bf16).astype(f32)
    t32[...] = jnp.zeros_like(t32)
    for v in range(8):
        t32[v, 5 * v:5 * v + 10, :] = fw
        t32[v, 126:127, :] = hi
        t32[v, 127:128, :] = b0[0:1] - hi
    t16[...] = t32[...].astype(bf16)
    pltpu.make_async_copy(t16, taps, osem.at[8]).start()
    ones = jnp.full((512, 128), 1.0 / 512, bf16)
    for b in range(8):
        fetch(b).wait()
        for i in range(4):
            at = slice(1024 * b + 256 * i, 1024 * b + 256 * i + 256)
            m = jnp.dot(raw[at, :], ones, preferred_element_type=f32)
            for c in range(4):
                k = slice(128 * c, 128 * c + 128)
                w[at, k] = (raw[at, k].astype(f32) - m).astype(bf16)
        leave(b).start()

    for k in range(4):
        @pl.when(jnp.logical_not(jnp.logical_and(mine, slot == k)))
        def _():
            pltpu.make_async_remote_copy(
                src_ref=held.at[0], dst_ref=out.at[k], send_sem=ssem.at[0], recv_sem=rsem.at[k],
                device_id=source(k), device_id_type=MESH).wait_recv()
    for e in range(2):
        for c in range(2):
            @pl.when(jnp.logical_not(here(e, c)))
            def _():
                copy(e, c).wait_send()

            @pl.when(here(e, c))
            def _():
                local(e, c).wait()
    pltpu.make_async_copy(t16, taps, osem.at[8]).wait()
    for b in range(8):
        leave(b).wait()


def exchange_audio(waves, first, mid, last, bias):
    bf16, f32 = jnp.bfloat16, jnp.float32
    return pl.pallas_call(
        audio_kernel,
        out_shape=(jax.ShapeDtypeStruct((4, 320, 128), bf16), jax.ShapeDtypeStruct((8192, 512), bf16),
                   jax.ShapeDtypeStruct((8, 128, 512), bf16), jax.ShapeDtypeStruct((7, 512), f32)),
        in_specs=[HBM, HBM, HBM, HBM, HBM],
        out_specs=(HBM, HBM, HBM, VM),
        scratch_shapes=[
            pltpu.VMEM((2, 40960), f32),
            pltpu.VMEM((10, 512), f32),
            pltpu.VMEM((7, 512), f32),
            pltpu.VMEM((2, 320, 128), f32),
            pltpu.VMEM((2, 320, 128), bf16),
            pltpu.VMEM((8192, 512), bf16),
            pltpu.VMEM((8192, 512), bf16),
            pltpu.VMEM((8, 128, 512), f32),
            pltpu.VMEM((8, 128, 512), bf16),
            pltpu.SemaphoreType.DMA((4,)),
            pltpu.SemaphoreType.DMA((4,)),
            pltpu.SemaphoreType.DMA((11,)),
            pltpu.SemaphoreType.DMA((9,)),
        ],
        compiler_params=pltpu.CompilerParams(collective_id=1, has_side_effects=True, vmem_limit_bytes=26 << 20),
        name="audio",
    )(*[pltpu.with_memory_space_constraint(x, pltpu.HBM) for x in (
        waves, first, mid.reshape(6144, 512), last.reshape(2048, 512), bias)])


def half_gelu(h):
    h = h.astype(jnp.bfloat16)
    u = jnp.minimum(h * h, jnp.bfloat16(6.25))
    q = jnp.bfloat16(QH[3])
    for c in QH[2::-1]:
        q = q * u + jnp.bfloat16(c)
    return h + h * jnp.tanh(h * q)


def finish(v, gain, shift):
    ss = jnp.sum(v * v, axis=-1, keepdims=True)
    r = lax.rsqrt(ss * (1.0 / 512) + EPS)
    return half_gelu((v * r) * gain + shift)


def encoder_kernel(lens, order, utts, taps, w, bias, gain, shift, pgain, pshift, out,
                   packed, lhs, y0, y1, e1, e2, e3, e4, e5, e6, halo, out32):
    f32, bf16 = jnp.float32, jnp.bfloat16
    seq = lax.axis_index("seq")
    own, core = seq // 2, seq % 2
    packed[...] = jnp.zeros_like(packed)
    lane = lax.broadcasted_iota(jnp.int32, (320, 128), 1)
    sample = lax.broadcasted_iota(jnp.int32, (320, 128), 0) * 128 + lane
    off = jnp.int32(0)
    for p in range(4):
        u = order[own, p]
        ln = lens[own, u]
        a, b = off // 128, off % 128
        part = jnp.where(sample < ln, utts[u].astype(f32), 0.0)
        rolled = pltpu.roll(part, b, 1)
        packed[pl.ds(a, 320), :] += jnp.where(lane >= b, rolled, 0.0)
        packed[pl.ds(a + 1, 320), :] += jnp.where(lane < b, rolled, 0.0)
        off = off + ln
    nv = ((off + 10239) // 10240 - core + 1) // 2

    def row(ref, l):
        return ref[pl.ds(l, 1), :]

    def dot_(a, b):
        return jnp.dot(a, b, preferred_element_type=f32)

    def epi(y, l, groups, dst):
        g, s = row(gain, l) * 0.5, row(shift, l) * 0.5
        b = row(bias, l)
        for k in range(groups):
            v = y[pl.ds(16 * k, 16), :]
            if l > 0:
                v = v + b
            dst(k, finish(v, g, s))

    def conv3(src, l, start, rows, gap, y):
        at = 1536 * l
        y[pl.ds(0, rows), :] = dot_(src[pl.ds(start, rows), :], w[at:at + 1024, :]) + dot_(
            src[pl.ds(start + gap, rows), 0:512], w[at + 1024:at + 1536, :])

    def put(ref, gap, base=0):
        def at(k, v):
            ref[pl.ds((k // 2) * gap + base, 16), (k % 2) * 512:(k % 2) * 512 + 512] = v
        return at

    lane16 = lax.broadcasted_iota(jnp.int32, (16, 128), 1)
    row16 = lax.broadcasted_iota(jnp.int32, (16, 512), 0)

    def windows(cols, count):
        for q in range(count):
            j, o = divmod(40 * q, 128)
            x = cols[j] if o == 0 else pltpu.roll(cols[j], 128 - o, 1)
            if o + 45 > 128:
                x = jnp.where(lane16 < 128 - o, x, pltpu.roll(cols[j + 1], 128 - o, 1))
            x = jnp.where(lane16 >= 126, 1.0, x)
            lhs[pl.ds(16 * q, 16), :] = x.astype(bf16)

    after = packed[pl.ds(80 * core + 80, 8, stride=160), :]
    windows([jnp.concatenate([after, jnp.zeros((8, 128), f32)], axis=0)], 2)
    for v in range(8):
        y0[pl.ds(32 * v, 32), :] = dot_(lhs[0:32, :], taps[v])

    def put_first(k, val):
        ph = 8 * (k % 2) + k // 2
        e1[pl.ds(16 * (ph // 2), 16), (ph % 2) * 512:(ph % 2) * 512 + 512] = val
    epi(y0, 0, 16, put_first)
    conv3(e1, 0, 0, 112, 16, y0)
    epi(y0, 1, 7, put(e2, 16))
    conv3(e2, 1, 0, 48, 16, y0)
    epi(y0, 2, 3, put(e3, 16))
    conv3(e3, 2, 0, 16, 16, y0)

    def keep4(k, val):
        halo[48:64, :] = val.astype(f32)
    epi(y0, 3, 1, keep4)
    for k, e in enumerate((e1, e2, e3)):
        halo[16 * k:16 * k + 16, :] = e[0:16, 0:512].astype(f32)
    silent = jnp.broadcast_to(halo[56:57, :], (16, 512)).astype(bf16)

    def fill(i, _):
        for k in range(17):
            e4[pl.ds((k // 2) * 128 + 16 * i, 16), (k % 2) * 512:(k % 2) * 512 + 512] = silent
        return 0
    lax.fori_loop(nv, 8, fill, 0)

    def wrap(e, l, i, first, last):
        x = pltpu.roll(e[pl.ds(first, 16), 0:512].astype(f32), 15, 0)
        x = jnp.where(row16 == 15, halo[pl.ds(16 * l + i, 1), :], x)
        e[pl.ds(last, 16), 0:512] = x.astype(bf16)

    def segment(i, _):
        base = 5 * (32 * i + 16 * core)
        windows([packed[pl.ds(base + j, 16, stride=5), :] for j in range(6)], 16)

        def first(v, y):
            y[...] = dot_(lhs[...], taps[v])

        def put1(v):
            def at(q, val):
                e1[pl.ds(64 * q + 16 * (v // 2), 16), 512 * (v % 2):512 * (v % 2) + 512] = val
            return at
        ys = (y0, y1)
        first(0, y0)
        for v in range(8):
            if v < 7:
                first(v + 1, ys[(v + 1) % 2])
            epi(ys[v % 2], 0, 16, put1(v))
        wrap(e1, 0, i, 0, 1024)
        conv3(e1, 0, 0, 256, 16, y0)
        conv3(e1, 0, 256, 256, 16, y1)
        epi(y0, 1, 16, put(e2, 16, 0))
        conv3(e1, 0, 512, 256, 16, y0)
        epi(y1, 1, 16, put(e2, 16, 128))
        conv3(e1, 0, 768, 256, 16, y1)
        epi(y0, 1, 16, put(e2, 16, 256))
        conv3(e2, 1, 0, 256, 16, y0)
        epi(y1, 1, 16, put(e2, 16, 384))
        wrap(e2, 1, i, 0, 512)
        conv3(e2, 1, 256, 256, 16, y1)
        epi(y0, 2, 16, put(e3, 16, 0))
        epi(y1, 2, 16, put(e3, 16, 128))
        wrap(e3, 2, i, 0, 256)
        conv3(e3, 2, 0, 256, 16, y0)
        at = pl.multiple_of(16 * i, 16)
        epi(y0, 3, 16, put(e4, 128, at))
        wrap(e4, 3, i, at, 1024 + at)
        return 0
    lax.fori_loop(0, nv, segment, 0)

    def conv2(src, l, start, y):
        y[...] = dot_(src[pl.ds(start, 256), :], w[6144 + 1024 * l:7168 + 1024 * l, :])

    def put8(ref, base):
        def at(k, v):
            ref[pl.ds(base + 16 * (k % 8), 16), (k // 8) * 512:(k // 8) * 512 + 512] = v
        return at
    conv3(e4, 3, 0, 256, 128, y0)
    conv3(e4, 3, 256, 256, 128, y1)
    epi(y0, 4, 16, put8(e5, 0))
    conv3(e4, 3, 512, 256, 128, y0)
    epi(y1, 4, 16, put8(e5, 128))
    conv3(e4, 3, 768, 256, 128, y1)
    epi(y0, 4, 16, put8(e5, 256))
    conv2(e5, 0, 0, y0)
    epi(y1, 4, 16, put8(e5, 384))
    conv2(e5, 0, 256, y1)
    epi(y0, 5, 16, put8(e6, 0))
    epi(y1, 5, 16, put8(e6, 128))
    conv2(e6, 1, 0, y0)
    pg, ps = pgain[...], pshift[...]

    def last(k, v):
        v = v.astype(f32)
        v = v - jnp.mean(v, axis=-1, keepdims=True)
        v = v * lax.rsqrt(jnp.mean(v * v, axis=-1, keepdims=True) + EPS) * pg + ps
        for c in range(4):
            out32[c, pl.ds(32 * (k % 8) + k // 8, 16, stride=2), :] = v[:, 128 * c:128 * c + 128]
    epi(y0, 6, 16, last)
    out[0:32, :] = jnp.zeros((32, 512), bf16)
    out[288:320, :] = jnp.zeros((32, 512), bf16)
    for c in range(4):
        out[32:288, 128 * c:128 * c + 128] = out32[c].astype(bf16)


def encode(lens, order, utts, taps, weights, bias, gain, shift, pgain, pshift):
    bf16, f32 = jnp.bfloat16, jnp.float32
    return pl.pallas_call(
        encoder_kernel,
        out_shape=jax.ShapeDtypeStruct((320, 512), bf16),
        in_specs=[SM, SM] + [VM] * 8,
        out_specs=VM,
        scratch_shapes=[
            pltpu.VMEM((1296, 128), f32),
            pltpu.VMEM((256, 128), bf16),
            pltpu.VMEM((256, 512), f32),
            pltpu.VMEM((256, 512), f32),
            pltpu.VMEM((65 * 16, 1024), bf16),
            pltpu.VMEM((33 * 16, 1024), bf16),
            pltpu.VMEM((17 * 16, 1024), bf16),
            pltpu.VMEM((9 * 128, 1024), bf16),
            pltpu.VMEM((4 * 128, 1024), bf16),
            pltpu.VMEM((2 * 128, 1024), bf16),
            pltpu.VMEM((64, 512), f32),
            pltpu.VMEM((4, 256, 128), f32),
        ],
        compiler_params=pltpu.CompilerParams(vmem_limit_bytes=30 << 20),
        name="encode",
    )(lens, order, utts, taps, weights, bias, gain, shift, pgain, pshift)


def frames_kernel(frames, out, ssem, rsem):
    seq = lax.axis_index("seq")
    barrier = pltpu.get_barrier_semaphore()
    for o in range(1, 8):
        pl.semaphore_signal(barrier, inc=1, device_id={"seq": (seq + o) % 8}, device_id_type=MESH)

    def piece(d):
        return frames.at[pl.ds(pl.multiple_of(32 * d + 32 * (1 - seq % 2), 32), 64)]

    def copy(o):
        d = (seq + o) % 8
        return pltpu.make_async_remote_copy(
            src_ref=piece(d), dst_ref=out.at[seq], send_sem=ssem.at[o], recv_sem=rsem.at[seq],
            device_id={"seq": d}, device_id_type=MESH)
    own = pltpu.make_async_copy(piece(seq), out.at[seq], ssem.at[0])
    own.start()
    pl.semaphore_wait(barrier, 7)
    for o in range(1, 8):
        copy(o).start()
    own.wait()
    for o in range(1, 8):
        d = (seq + o) % 8
        pltpu.make_async_remote_copy(
            src_ref=piece(d), dst_ref=out.at[d], send_sem=ssem.at[o], recv_sem=rsem.at[d],
            device_id={"seq": d}, device_id_type=MESH).wait_recv()
    for o in range(1, 8):
        copy(o).wait_send()


def exchange_frames(frames):
    return pl.pallas_call(
        frames_kernel,
        out_shape=jax.ShapeDtypeStruct((8, 64, 512), jnp.bfloat16),
        in_specs=[HBM],
        out_specs=HBM,
        scratch_shapes=[pltpu.SemaphoreType.DMA((8,)), pltpu.SemaphoreType.DMA((8,))],
        compiler_params=pltpu.CompilerParams(collective_id=2, has_side_effects=True, vmem_limit_bytes=1 << 20),
        name="frames",
    )(frames)


def conformer_kernel(lens, recv, wp, pb, gain, up, taps, dbias, down, out,
                     nrm, s0, s1, lifted, ya, yb, g, act):
    f32, bf16 = jnp.float32, jnp.bfloat16
    base = 64 * lax.axis_index("seq") - 32
    for r in range(4):
        for c in range(4):
            nrm[128 * r + 32 * c:128 * r + 32 * c + 32, :] = recv[2 * r + (c + 1) % 2, 32 * (c // 2):32 * (c // 2) + 32, :]

    def dot_(a, b):
        return jnp.dot(a, b, preferred_element_type=f32)

    halves = (slice(0, 512), slice(512, 1024))
    for w in halves:
        s0[:, w] = dot_(nrm[...], wp[:, w]) + pb[:, w]

    def norm(src, l, rows):
        gl = gain[l:l + 1, :]

        def body(i, _):
            at = pl.ds(pl.multiple_of(16 * i, 16), 16)
            v = src[at, :]
            v = v - jnp.mean(v, axis=-1, keepdims=True)
            v = v * lax.rsqrt(jnp.mean(v * v, axis=-1, keepdims=True) + EPS) * gl
            lifted[at, :] = v.astype(bf16)
            return 0
        lax.fori_loop(0, rows // 16, body, 0, unroll=8)

    def module(l, per, lo, keep):
        rows = 4 * per
        first = 64 - keep // 2
        ahead = base + lo + lax.broadcasted_iota(jnp.int32, (16, 128), 0)

        def lift(n):
            ya[0:rows, :] = dot_(lifted[0:rows, :], up[l, :, 512 * n:512 * n + 512])
            yb[0:rows, :] = dot_(lifted[0:rows, :], up[l, :, 1024 + 512 * n:1536 + 512 * n])

        def gate(n):
            for r in range(4):
                total = lens[r, 0] + lens[r, 1] + lens[r, 2] + lens[r, 3]
                valid = (total - 400) // 320 + 1
                for k in range(per // 16):
                    at = slice(per * r + 16 * k, per * r + 16 * k + 16)
                    t = ahead + 16 * k
                    live = jnp.logical_and(t >= 0, t < valid)
                    for c in range(4):
                        w = slice(128 * c, 128 * c + 128)
                        v = ya[at, w] * jax.nn.sigmoid(yb[at, w])
                        g[4 * n + c, r, lo + 16 * k:lo + 16 * k + 16, :] = jnp.where(live, v, 0.0)

        def block(c, r, w):
            acc = jnp.broadcast_to(dbias[l:l + 1, w], (keep, 128))
            for j in range(31):
                acc = acc + g[c, r, first + j - 15:first + j - 15 + keep, :] * taps[j, l:l + 1, w]
            act[keep * r:keep * r + keep, w] = (acc * jax.nn.sigmoid(acc)).astype(bf16)

        def depth(c, _):
            for r in range(4):
                block(c, r, pl.ds(pl.multiple_of(128 * c, 128), 128))
            return 0
        lift(0)
        gate(0)
        lift(1)
        gate(1)
        lax.fori_loop(0, 8, depth, 0)

    norm(s0, 0, 512)
    module(0, 128, 0, 96)
    for w in halves:
        d = dot_(act[...], down[0, :, w])
        for r in range(4):
            s1[96 * r:96 * r + 96, w] = s0[128 * r + 16:128 * r + 112, w] + d[96 * r:96 * r + 96]
    norm(s1, 1, 384)
    module(1, 96, 16, 64)
    for w in halves:
        d = dot_(act[0:256, :], down[1, :, w])
        for r in range(4):
            out[r, :, w] = (s1[96 * r + 16:96 * r + 80, w] + d[64 * r:64 * r + 64]).astype(bf16)


def conform(lens, recv, wp, pb, gain, up, taps, dbias, down):
    bf16, f32 = jnp.bfloat16, jnp.float32
    return pl.pallas_call(
        conformer_kernel,
        out_shape=jax.ShapeDtypeStruct((4, 64, 1024), bf16),
        in_specs=[SM] + [VM] * 8,
        out_specs=VM,
        scratch_shapes=[
            pltpu.VMEM((512, 512), bf16),
            pltpu.VMEM((512, 1024), f32),
            pltpu.VMEM((384, 1024), f32),
            pltpu.VMEM((512, 1024), bf16),
            pltpu.VMEM((512, 512), f32),
            pltpu.VMEM((512, 512), f32),
            pltpu.VMEM((8, 4, 128, 128), f32),
            pltpu.VMEM((384, 1024), bf16),
        ],
        compiler_params=pltpu.CompilerParams(vmem_limit_bytes=20 << 20),
        name="conform",
    )(lens, recv, wp, pb, gain, up, jnp.transpose(taps, (1, 0, 2)), dbias, down)


def per_device(waveforms, utt_len, pack_order, conv_first, conv_mid, conv_last, conv_bias, conv_gain,
               conv_shift, proj_gain, proj_shift, proj_weight, proj_bias, conf_gain, conf_up,
               conf_depth, depth_bias, conf_down):
    utts, weights, taps, bias = exchange_audio(waveforms, conv_first, conv_mid, conv_last, conv_bias)
    frames = encode(utt_len, pack_order, utts, taps, weights, bias, conv_gain, conv_shift,
                    proj_gain[None], proj_shift[None])
    recv = exchange_frames(frames)
    return conform(utt_len, recv, proj_weight, proj_bias[None], conf_gain, conf_up, conf_depth,
                   depth_bias, conf_down)


def solution(mesh):
    return jax.shard_map(
        per_device,
        mesh=mesh,
        in_specs=(P(("dp", "seq"), None), P("dp", None), P("dp", None)) + (P(),) * 15,
        out_specs=P("dp", "seq", None),
        check_vma=False,
    )
```

```python
import jax
import jax.numpy as jnp
from jax import lax
from jax.experimental import pallas as pl
from jax.experimental.pallas import tpu as pltpu
from jax.sharding import PartitionSpec as P

EPS = 1e-05
QH = tuple(2.0 * c * 4.0 ** i for i, c in enumerate((0.7976911, 0.03672923, -0.00025450048, -8.666277e-06)))
MESH = pl.DeviceIdType.MESH
VM = pl.BlockSpec(memory_space=pltpu.VMEM)
SM = pl.BlockSpec(memory_space=pltpu.SMEM)
ANY = pl.BlockSpec(memory_space=pl.ANY)
HBM = pl.BlockSpec(memory_space=pltpu.HBM)


def audio_kernel(waves_in, first_in, mid, last, bias_in, out, weights, taps, bias,
                 waves, first, bias_raw, stage, held, raw, w, t32, t16, ssem, rsem, wsem, osem):
    f32, bf16 = jnp.float32, jnp.bfloat16
    dp, seq = lax.axis_index("dp"), lax.axis_index("seq")
    mine = seq == dp // 2
    barrier = pltpu.get_barrier_semaphore()

    def source(k):
        return {"dp": 4 * (seq // 2) + k, "seq": dp // 2}

    for k in range(4):
        @pl.when(jnp.logical_not(jnp.logical_and(mine, dp % 4 == k)))
        def _():
            pl.semaphore_signal(barrier, inc=1, device_id=source(k), device_id_type=MESH)

    def fetch(b):
        src = mid.at[pl.ds(1024 * b, 1024)] if b < 6 else last.at[pl.ds(1024 * (b - 6), 1024)]
        return pltpu.make_async_copy(src, raw.at[pl.ds(1024 * b, 1024)], wsem.at[b])

    def leave(b):
        at = pl.ds(1024 * b, 1024)
        return pltpu.make_async_copy(w.at[at], weights.at[at], osem.at[b])

    small = [pltpu.make_async_copy(x, y, wsem.at[8 + k]) for k, (x, y) in enumerate(
        ((waves_in, waves), (first_in, first), (bias_in, bias_raw)))]
    for c in small:
        c.start()
    for b in range(8):
        fetch(b).start()
    small[0].wait()

    def unfold(i, _):
        for e in range(2):
            stage[e, pl.ds(i, 1), :] = waves[e:e + 1, pl.ds(pl.multiple_of(128 * i, 128), 128)]
        return 0
    lax.fori_loop(0, 320, unfold, 0, unroll=8)
    held[...] = stage[...].astype(bf16)
    pl.semaphore_wait(barrier, jnp.where(mine, 3, 4))
    slot = dp % 4

    def copy(e, c):
        return pltpu.make_async_remote_copy(
            src_ref=held.at[e], dst_ref=out.at[slot],
            send_sem=ssem.at[2 * e + c], recv_sem=rsem.at[slot],
            device_id={"dp": 2 * seq + e, "seq": 2 * (dp // 4) + c}, device_id_type=MESH)

    def here(e, c):
        return jnp.logical_and(mine, jnp.logical_and(dp % 2 == e, seq % 2 == c))

    def local(e, c):
        return pltpu.make_async_copy(held.at[e], out.at[slot], ssem.at[2 * e + c])

    for e in range(2):
        for c in range(2):
            @pl.when(jnp.logical_not(here(e, c)))
            def _():
                copy(e, c).start()

            @pl.when(here(e, c))
            def _():
                local(e, c).start()

    small[1].wait()
    small[2].wait()
    b0 = bias_raw[...] - jnp.mean(bias_raw[...], axis=-1, keepdims=True)
    bias[...] = b0
    fw = first[...] - jnp.mean(first[...], axis=-1, keepdims=True)
    hi = b0[0:1].astype(bf16).astype(f32)
    t32[...] = jnp.zeros_like(t32)
    for v in range(4):
        t32[v, 5 * v:5 * v + 10, :] = fw
        t32[v, 126:127, :] = hi
        t32[v, 127:128, :] = b0[0:1] - hi
    t16[...] = t32[...].astype(bf16)
    pltpu.make_async_copy(t16, taps, osem.at[8]).start()
    ones = jnp.full((512, 128), 1.0 / 512, bf16)
    for b in range(8):
        fetch(b).wait()
        for i in range(4):
            at = slice(1024 * b + 256 * i, 1024 * b + 256 * i + 256)
            m = jnp.dot(raw[at, :], ones, preferred_element_type=f32)
            for c in range(4):
                k = slice(128 * c, 128 * c + 128)
                w[at, k] = (raw[at, k].astype(f32) - m).astype(bf16)
        leave(b).start()

    for k in range(4):
        @pl.when(jnp.logical_not(jnp.logical_and(mine, slot == k)))
        def _():
            pltpu.make_async_remote_copy(
                src_ref=held.at[0], dst_ref=out.at[k], send_sem=ssem.at[0], recv_sem=rsem.at[k],
                device_id=source(k), device_id_type=MESH).wait_recv()
    for e in range(2):
        for c in range(2):
            @pl.when(jnp.logical_not(here(e, c)))
            def _():
                copy(e, c).wait_send()

            @pl.when(here(e, c))
            def _():
                local(e, c).wait()
    pltpu.make_async_copy(t16, taps, osem.at[8]).wait()
    for b in range(8):
        leave(b).wait()


def exchange_audio(waves, first, mid, last, bias):
    bf16, f32 = jnp.bfloat16, jnp.float32
    return pl.pallas_call(
        audio_kernel,
        out_shape=(jax.ShapeDtypeStruct((4, 320, 128), bf16), jax.ShapeDtypeStruct((8192, 512), bf16),
                   jax.ShapeDtypeStruct((4, 128, 512), bf16), jax.ShapeDtypeStruct((7, 512), f32)),
        in_specs=[HBM, HBM, HBM, HBM, HBM],
        out_specs=(HBM, HBM, HBM, VM),
        scratch_shapes=[
            pltpu.VMEM((2, 40960), f32),
            pltpu.VMEM((10, 512), f32),
            pltpu.VMEM((7, 512), f32),
            pltpu.VMEM((2, 320, 128), f32),
            pltpu.VMEM((2, 320, 128), bf16),
            pltpu.VMEM((8192, 512), bf16),
            pltpu.VMEM((8192, 512), bf16),
            pltpu.VMEM((4, 128, 512), f32),
            pltpu.VMEM((4, 128, 512), bf16),
            pltpu.SemaphoreType.DMA((4,)),
            pltpu.SemaphoreType.DMA((4,)),
            pltpu.SemaphoreType.DMA((11,)),
            pltpu.SemaphoreType.DMA((9,)),
        ],
        compiler_params=pltpu.CompilerParams(collective_id=1, has_side_effects=True, vmem_limit_bytes=26 << 20),
        name="audio",
    )(*[pltpu.with_memory_space_constraint(x, pltpu.HBM) for x in (
        waves, first, mid.reshape(6144, 512), last.reshape(2048, 512), bias)])


def half_gelu(h):
    h = h.astype(jnp.bfloat16)
    u = jnp.minimum(h * h, jnp.bfloat16(6.25))
    q = jnp.bfloat16(QH[3])
    for c in QH[2::-1]:
        q = q * u + jnp.bfloat16(c)
    return h + h * jnp.tanh(h * q)


def finish(v, gain, shift):
    ss = jnp.sum(v * v, axis=-1, keepdims=True)
    r = lax.rsqrt(ss * (1.0 / 512) + EPS)
    return half_gelu((v * r) * gain + shift)


class Held:
    v = None


def encoder_kernel(lens, order, utts, taps, w, bias, gain, shift, pgain, pshift, out,
                   packed, lhs, y0, y1, e1, e2, e3, e4, e5, e6, halo, out32):
    f32, bf16 = jnp.float32, jnp.bfloat16
    seq = lax.axis_index("seq")
    own, core = seq // 2, seq % 2
    packed[...] = jnp.zeros_like(packed)
    lane = lax.broadcasted_iota(jnp.int32, (320, 128), 1)
    sample = lax.broadcasted_iota(jnp.int32, (320, 128), 0) * 128 + lane
    off = jnp.int32(0)
    for p in range(4):
        u = order[own, p]
        ln = lens[own, u]
        a, b = off // 128, off % 128
        part = jnp.where(sample < ln, utts[u].astype(f32), 0.0)
        rolled = pltpu.roll(part, b, 1)
        packed[pl.ds(a, 320), :] += jnp.where(lane >= b, rolled, 0.0)
        packed[pl.ds(a + 1, 320), :] += jnp.where(lane < b, rolled, 0.0)
        off = off + ln
    nv = ((off + 10239) // 10240 - core + 1) // 2

    def row(ref, l):
        return ref[pl.ds(l, 1), :]

    def dot_(a, b):
        return jnp.dot(a, b, preferred_element_type=f32)

    def epi(y, l, groups, dst, nxt=None):
        g, s = row(gain, l) * 0.5, row(shift, l) * 0.5
        b = row(bias, l)
        for k in range(groups):
            if k % 8 == 0 and isinstance(y, Held):
                if len(y.v) <= k // 8:
                    y.v.append(y.jobs.pop(0)())
                if nxt is not None and nxt.jobs:
                    nxt.v.append(nxt.jobs.pop(0)())
            v = y.v[k // 8][16 * (k % 8):16 * (k % 8) + 16] if isinstance(y, Held) else y[pl.ds(16 * k, 16), :]
            if l > 0:
                v = v + b
            dst(k, finish(v, g, s))

    def conv3(src, l, start, rows, gap, y):
        at = 1536 * l
        if not isinstance(y, Held):
            y[pl.ds(0, rows), :] = dot_(src[pl.ds(start, rows), :], w[at:at + 1024, :]) + dot_(
                src[pl.ds(start + gap, rows), 0:512], w[at + 1024:at + 1536, :])
            return
        y.v, y.jobs = [], [lambda o=o: dot_(src[pl.ds(start + o, 128), :], w[at:at + 1024, :]) + dot_(
            src[pl.ds(start + gap + o, 128), 0:512], w[at + 1024:at + 1536, :]) for o in range(0, rows, 128)]

    def put(ref, gap, base=0):
        def at(k, v):
            ref[pl.ds((k // 2) * gap + base, 16), (k % 2) * 512:(k % 2) * 512 + 512] = v
        return at

    lane16 = lax.broadcasted_iota(jnp.int32, (16, 128), 1)
    row16 = lax.broadcasted_iota(jnp.int32, (16, 512), 0)

    def windows(cols, count):
        for q in range(count):
            j, o = divmod(20 * q, 128)
            x = cols[j] if o == 0 else pltpu.roll(cols[j], 128 - o, 1)
            if o + 25 > 128:
                x = jnp.where(lane16 < 128 - o, x, pltpu.roll(cols[j + 1], 128 - o, 1))
            x = jnp.where(lane16 >= 126, 1.0, x)
            lhs[pl.ds(16 * q, 16), :] = x.astype(bf16)

    after = packed[pl.ds(80 * core + 80, 8, stride=160), :]
    windows([jnp.concatenate([after, jnp.zeros((8, 128), f32)], axis=0)], 4)
    for v in range(4):
        y0[pl.ds(64 * v, 64), :] = dot_(lhs[0:64, :], taps[v])

    def put_first(k, val):
        ph = 4 * (k % 4) + k // 4
        e1[pl.ds(16 * (ph // 2), 16), (ph % 2) * 512:(ph % 2) * 512 + 512] = val
    epi(y0, 0, 16, put_first)
    conv3(e1, 0, 0, 112, 16, y0)
    epi(y0, 1, 7, put(e2, 16))
    conv3(e2, 1, 0, 48, 16, y0)
    epi(y0, 2, 3, put(e3, 16))
    conv3(e3, 2, 0, 16, 16, y0)

    def keep4(k, val):
        halo[48:64, :] = val.astype(f32)
    epi(y0, 3, 1, keep4)
    for k, e in enumerate((e1, e2, e3)):
        halo[16 * k:16 * k + 16, :] = e[0:16, 0:512].astype(f32)
    silent = jnp.broadcast_to(halo[56:57, :], (16, 512)).astype(bf16)

    def fill(i, _):
        for k in range(17):
            e4[pl.ds((k // 2) * 128 + 16 * i, 16), (k % 2) * 512:(k % 2) * 512 + 512] = silent
        return 0
    lax.fori_loop(nv, 8, fill, 0)

    def wrap(e, l, i, first, last):
        x = pltpu.roll(e[pl.ds(first, 16), 0:512].astype(f32), 15, 0)
        x = jnp.where(row16 == 15, halo[pl.ds(16 * l + i, 1), :], x)
        e[pl.ds(last, 16), 0:512] = x.astype(bf16)

    def segment(i, _):
        base = 5 * (32 * i + 16 * core)
        windows([packed[pl.ds(base + j, 16, stride=5), :] for j in range(6)], 32)
        y0, y1 = Held(), Held()

        def first(v, y):
            y.v, y.jobs = [], [lambda o=o: dot_(lhs[o:o + 128, :], taps[v]) for o in range(0, 512, 128)]

        def put1(v):
            def at(q, val):
                e1[pl.ds(32 * q + 16 * (v // 2), 16), 512 * (v % 2):512 * (v % 2) + 512] = val
            return at
        ys = (y0, y1)
        first(0, y0)
        for v in range(4):
            if v < 3:
                first(v + 1, ys[(v + 1) % 2])
            epi(ys[v % 2], 0, 32, put1(v), ys[(v + 1) % 2] if v < 3 else None)
        wrap(e1, 0, i, 0, 1024)
        conv3(e1, 0, 0, 256, 16, y0)
        conv3(e1, 0, 256, 256, 16, y1)
        epi(y0, 1, 16, put(e2, 16, 0), y1)
        conv3(e1, 0, 512, 256, 16, y0)
        epi(y1, 1, 16, put(e2, 16, 128), y0)
        conv3(e1, 0, 768, 256, 16, y1)
        epi(y0, 1, 16, put(e2, 16, 256), y1)
        conv3(e2, 1, 0, 256, 16, y0)
        epi(y1, 1, 16, put(e2, 16, 384), y0)
        wrap(e2, 1, i, 0, 512)
        conv3(e2, 1, 256, 256, 16, y1)
        epi(y0, 2, 16, put(e3, 16, 0), y1)
        epi(y1, 2, 16, put(e3, 16, 128))
        wrap(e3, 2, i, 0, 256)
        conv3(e3, 2, 0, 256, 16, y0)
        at = pl.multiple_of(16 * i, 16)
        epi(y0, 3, 16, put(e4, 128, at))
        wrap(e4, 3, i, at, 1024 + at)
        return 0
    lax.fori_loop(0, nv, segment, 0)

    def conv2(src, l, start, y):
        y.v, y.jobs = [], [lambda o=o: dot_(src[pl.ds(start + o, 128), :], w[6144 + 1024 * l:7168 + 1024 * l, :]) for o in (0, 128)]

    def put8(ref, base):
        def at(k, v):
            ref[pl.ds(base + 16 * (k % 8), 16), (k // 8) * 512:(k // 8) * 512 + 512] = v
        return at
    y0, y1 = Held(), Held()
    conv3(e4, 3, 0, 256, 128, y0)
    conv3(e4, 3, 256, 256, 128, y1)
    epi(y0, 4, 16, put8(e5, 0), y1)
    conv3(e4, 3, 512, 256, 128, y0)
    epi(y1, 4, 16, put8(e5, 128), y0)
    conv3(e4, 3, 768, 256, 128, y1)
    epi(y0, 4, 16, put8(e5, 256), y1)
    conv2(e5, 0, 0, y0)
    epi(y1, 4, 16, put8(e5, 384), y0)
    conv2(e5, 0, 256, y1)
    epi(y0, 5, 16, put8(e6, 0), y1)
    epi(y1, 5, 16, put8(e6, 128))
    conv2(e6, 1, 0, y0)
    pg, ps = pgain[...], pshift[...]

    def last(k, v):
        v = v.astype(f32)
        v = v - jnp.mean(v, axis=-1, keepdims=True)
        v = v * lax.rsqrt(jnp.mean(v * v, axis=-1, keepdims=True) + EPS) * pg + ps
        for c in range(4):
            out32[c, pl.ds(32 * (k % 8) + k // 8, 16, stride=2), :] = v[:, 128 * c:128 * c + 128]
    epi(y0, 6, 16, last)
    out[0:32, :] = jnp.zeros((32, 512), bf16)
    out[288:320, :] = jnp.zeros((32, 512), bf16)
    for c in range(4):
        out[32:288, 128 * c:128 * c + 128] = out32[c].astype(bf16)


def encode(lens, order, utts, taps, weights, bias, gain, shift, pgain, pshift):
    bf16, f32 = jnp.bfloat16, jnp.float32
    return pl.pallas_call(
        encoder_kernel,
        out_shape=jax.ShapeDtypeStruct((320, 512), bf16),
        in_specs=[SM, SM] + [VM] * 8,
        out_specs=VM,
        scratch_shapes=[
            pltpu.VMEM((1296, 128), f32),
            pltpu.VMEM((512, 128), bf16),
            pltpu.VMEM((512, 512), f32),
            pltpu.VMEM((512, 512), f32),
            pltpu.VMEM((65 * 16, 1024), bf16),
            pltpu.VMEM((33 * 16, 1024), bf16),
            pltpu.VMEM((17 * 16, 1024), bf16),
            pltpu.VMEM((9 * 128, 1024), bf16),
            pltpu.VMEM((4 * 128, 1024), bf16),
            pltpu.VMEM((2 * 128, 1024), bf16),
            pltpu.VMEM((64, 512), f32),
            pltpu.VMEM((4, 256, 128), f32),
        ],
        compiler_params=pltpu.CompilerParams(vmem_limit_bytes=30 << 20),
        name="encode",
    )(lens, order, utts, taps, weights, bias, gain, shift, pgain, pshift)


def frames_kernel(frames, out, ssem, rsem):
    seq = lax.axis_index("seq")
    barrier = pltpu.get_barrier_semaphore()
    for o in range(1, 8):
        pl.semaphore_signal(barrier, inc=1, device_id={"seq": (seq + o) % 8}, device_id_type=MESH)

    def piece(d):
        return frames.at[pl.ds(pl.multiple_of(32 * d + 32 * (1 - seq % 2), 32), 64)]

    def copy(o):
        d = (seq + o) % 8
        return pltpu.make_async_remote_copy(
            src_ref=piece(d), dst_ref=out.at[seq], send_sem=ssem.at[o], recv_sem=rsem.at[seq],
            device_id={"seq": d}, device_id_type=MESH)
    own = pltpu.make_async_copy(piece(seq), out.at[seq], ssem.at[0])
    own.start()
    pl.semaphore_wait(barrier, 7)
    for o in range(1, 8):
        copy(o).start()
    own.wait()
    for o in range(1, 8):
        d = (seq + o) % 8
        pltpu.make_async_remote_copy(
            src_ref=piece(d), dst_ref=out.at[d], send_sem=ssem.at[o], recv_sem=rsem.at[d],
            device_id={"seq": d}, device_id_type=MESH).wait_recv()
    for o in range(1, 8):
        copy(o).wait_send()


def exchange_frames(frames):
    return pl.pallas_call(
        frames_kernel,
        out_shape=jax.ShapeDtypeStruct((8, 64, 512), jnp.bfloat16),
        in_specs=[HBM],
        out_specs=HBM,
        scratch_shapes=[pltpu.SemaphoreType.DMA((8,)), pltpu.SemaphoreType.DMA((8,))],
        compiler_params=pltpu.CompilerParams(collective_id=2, has_side_effects=True, vmem_limit_bytes=1 << 20),
        name="frames",
    )(frames)


def conformer_kernel(lens, recv, wp, pb, gain, up, taps, dbias, down, out,
                     nrm, s0, s1, lifted, ya, yb, g, act):
    f32, bf16 = jnp.float32, jnp.bfloat16
    base = 64 * lax.axis_index("seq") - 32
    for r in range(4):
        for c in range(4):
            nrm[128 * r + 32 * c:128 * r + 32 * c + 32, :] = recv[2 * r + (c + 1) % 2, 32 * (c // 2):32 * (c // 2) + 32, :]

    def dot_(a, b):
        return jnp.dot(a, b, preferred_element_type=f32)

    halves = (slice(0, 512), slice(512, 1024))
    for w in halves:
        s0[:, w] = dot_(nrm[...], wp[:, w]) + pb[:, w]

    def norm(src, l, rows):
        gl = gain[l:l + 1, :]

        def body(i, _):
            at = pl.ds(pl.multiple_of(16 * i, 16), 16)
            v = src[at, :]
            v = v - jnp.mean(v, axis=-1, keepdims=True)
            v = v * lax.rsqrt(jnp.mean(v * v, axis=-1, keepdims=True) + EPS) * gl
            lifted[at, :] = v.astype(bf16)
            return 0
        lax.fori_loop(0, rows // 16, body, 0, unroll=True)

    def module(l, per, lo, keep):
        rows = 4 * per
        first = 64 - keep // 2
        ahead = base + lo + lax.broadcasted_iota(jnp.int32, (16, 128), 0)

        def lift(n):
            ya[0:rows, :] = dot_(lifted[0:rows, :], up[l, :, 512 * n:512 * n + 512])
            yb[0:rows, :] = dot_(lifted[0:rows, :], up[l, :, 1024 + 512 * n:1536 + 512 * n])

        def gate(n):
            for r in range(4):
                total = lens[r, 0] + lens[r, 1] + lens[r, 2] + lens[r, 3]
                valid = (total - 400) // 320 + 1
                for k in range(per // 16):
                    at = slice(per * r + 16 * k, per * r + 16 * k + 16)
                    t = ahead + 16 * k
                    live = jnp.logical_and(t >= 0, t < valid)
                    for c in range(4):
                        w = slice(128 * c, 128 * c + 128)
                        v = ya[at, w] * jax.nn.sigmoid(yb[at, w])
                        g[4 * n + c, r, lo + 16 * k:lo + 16 * k + 16, :] = jnp.where(live, v, 0.0)

        def block(c, r, w):
            acc = jnp.broadcast_to(dbias[l:l + 1, w], (keep, 128))
            for j in range(31):
                acc = acc + g[c, r, first + j - 15:first + j - 15 + keep, :] * taps[j, l:l + 1, w]
            act[keep * r:keep * r + keep, w] = (acc * jax.nn.sigmoid(acc)).astype(bf16)

        def depth(c, _):
            for r in range(4):
                block(c, r, pl.ds(pl.multiple_of(128 * c, 128), 128))
            return 0
        lift(0)
        gate(0)
        lift(1)
        gate(1)
        lax.fori_loop(0, 8, depth, 0)

    norm(s0, 0, 512)
    module(0, 128, 0, 96)
    for w in halves:
        d = dot_(act[...], down[0, :, w])
        for r in range(4):
            s1[96 * r:96 * r + 96, w] = s0[128 * r + 16:128 * r + 112, w] + d[96 * r:96 * r + 96]
    norm(s1, 1, 384)
    module(1, 96, 16, 64)
    for w in halves:
        d = dot_(act[0:256, :], down[1, :, w])
        for r in range(4):
            out[r, :, w] = (s1[96 * r + 16:96 * r + 80, w] + d[64 * r:64 * r + 64]).astype(bf16)


def conform(lens, recv, wp, pb, gain, up, taps, dbias, down):
    bf16, f32 = jnp.bfloat16, jnp.float32
    return pl.pallas_call(
        conformer_kernel,
        out_shape=jax.ShapeDtypeStruct((4, 64, 1024), bf16),
        in_specs=[SM] + [VM] * 8,
        out_specs=VM,
        scratch_shapes=[
            pltpu.VMEM((512, 512), bf16),
            pltpu.VMEM((512, 1024), f32),
            pltpu.VMEM((384, 1024), f32),
            pltpu.VMEM((512, 1024), bf16),
            pltpu.VMEM((512, 512), f32),
            pltpu.VMEM((512, 512), f32),
            pltpu.VMEM((8, 4, 128, 128), f32),
            pltpu.VMEM((384, 1024), bf16),
        ],
        compiler_params=pltpu.CompilerParams(vmem_limit_bytes=20 << 20),
        name="conform",
    )(lens, recv, wp, pb, gain, up, jnp.transpose(taps, (1, 0, 2)), dbias, down)


def per_device(waveforms, utt_len, pack_order, conv_first, conv_mid, conv_last, conv_bias, conv_gain,
               conv_shift, proj_gain, proj_shift, proj_weight, proj_bias, conf_gain, conf_up,
               conf_depth, depth_bias, conf_down):
    utts, weights, taps, bias = exchange_audio(waveforms, conv_first, conv_mid, conv_last, conv_bias)
    frames = encode(utt_len, pack_order, utts, taps, weights, bias, conv_gain, conv_shift,
                    proj_gain[None], proj_shift[None])
    recv = exchange_frames(frames)
    return conform(utt_len, recv, proj_weight, proj_bias[None], conf_gain, conf_up, conf_depth,
                   depth_bias, conf_down)


def solution(mesh):
    return jax.shard_map(
        per_device,
        mesh=mesh,
        in_specs=(P(("dp", "seq"), None), P("dp", None), P("dp", None)) + (P(),) * 15,
        out_specs=P("dp", "seq", None),
        check_vma=False,
    )
```

```python
import jax
import jax.numpy as jnp
from jax import lax
from jax.experimental import pallas as pl
from jax.experimental.pallas import tpu as pltpu
from jax.sharding import PartitionSpec as P

EPS = 1e-05
QH = tuple(2.0 * c * 4.0 ** i for i, c in enumerate((0.7976911, 0.03672923, -0.00025450048, -8.666277e-06)))
MESH = pl.DeviceIdType.MESH
VM = pl.BlockSpec(memory_space=pltpu.VMEM)
SM = pl.BlockSpec(memory_space=pltpu.SMEM)
ANY = pl.BlockSpec(memory_space=pl.ANY)
HBM = pl.BlockSpec(memory_space=pltpu.HBM)


def audio_kernel(waves_in, first_in, mid, last, bias_in, out, weights, taps, bias,
                 waves, first, bias_raw, stage, held, raw, t32, ssem, rsem, wsem):
    f32, bf16 = jnp.float32, jnp.bfloat16
    dp, seq = lax.axis_index("dp"), lax.axis_index("seq")
    mine = seq == dp // 2
    barrier = pltpu.get_barrier_semaphore()

    def source(k):
        return {"dp": 4 * (seq // 2) + k, "seq": dp // 2}

    for k in range(4):
        @pl.when(jnp.logical_not(jnp.logical_and(mine, dp % 4 == k)))
        def _():
            pl.semaphore_signal(barrier, inc=1, device_id=source(k), device_id_type=MESH)

    def fetch(b):
        src = mid.at[pl.ds(1024 * b, 1024)] if b < 6 else last.at[pl.ds(1024 * (b - 6), 1024)]
        return pltpu.make_async_copy(src, raw.at[pl.ds(1024 * b, 1024)], wsem.at[b])

    small = [pltpu.make_async_copy(x, y, wsem.at[8 + k]) for k, (x, y) in enumerate(
        ((waves_in, waves), (first_in, first), (bias_in, bias_raw)))]
    for c in small:
        c.start()
    for b in range(8):
        fetch(b).start()
    small[0].wait()

    def unfold(i, _):
        for e in range(2):
            stage[e, pl.ds(i, 1), :] = waves[e:e + 1, pl.ds(pl.multiple_of(128 * i, 128), 128)]
        return 0
    lax.fori_loop(0, 320, unfold, 0, unroll=8)
    held[...] = stage[...].astype(bf16)
    pl.semaphore_wait(barrier, jnp.where(mine, 3, 4))
    slot = dp % 4

    def copy(e, c):
        return pltpu.make_async_remote_copy(
            src_ref=held.at[e], dst_ref=out.at[slot],
            send_sem=ssem.at[2 * e + c], recv_sem=rsem.at[slot],
            device_id={"dp": 2 * seq + e, "seq": 2 * (dp // 4) + c}, device_id_type=MESH)

    def here(e, c):
        return jnp.logical_and(mine, jnp.logical_and(dp % 2 == e, seq % 2 == c))

    def local(e, c):
        return pltpu.make_async_copy(held.at[e], out.at[slot], ssem.at[2 * e + c])

    for e in range(2):
        for c in range(2):
            @pl.when(jnp.logical_not(here(e, c)))
            def _():
                copy(e, c).start()

            @pl.when(here(e, c))
            def _():
                local(e, c).start()

    small[1].wait()
    small[2].wait()
    b0 = bias_raw[...] - jnp.mean(bias_raw[...], axis=-1, keepdims=True)
    bias[...] = b0
    fw = first[...] - jnp.mean(first[...], axis=-1, keepdims=True)
    hi = b0[0:1].astype(bf16).astype(f32)
    t32[...] = jnp.zeros_like(t32)
    for v in range(4):
        t32[v, 5 * v:5 * v + 10, :] = fw
        t32[v, 126:127, :] = hi
        t32[v, 127:128, :] = b0[0:1] - hi
    taps[...] = t32[...].astype(bf16)
    ones = jnp.full((512, 128), 1.0 / 512, bf16)
    for b in range(8):
        fetch(b).wait()
        for i in range(4):
            at = slice(1024 * b + 256 * i, 1024 * b + 256 * i + 256)
            m = jnp.dot(raw[at, :], ones, preferred_element_type=f32)
            for c in range(4):
                k = slice(128 * c, 128 * c + 128)
                weights[at, k] = (raw[at, k].astype(f32) - m).astype(bf16)

    for k in range(4):
        @pl.when(jnp.logical_not(jnp.logical_and(mine, slot == k)))
        def _():
            pltpu.make_async_remote_copy(
                src_ref=held.at[0], dst_ref=out.at[k], send_sem=ssem.at[0], recv_sem=rsem.at[k],
                device_id=source(k), device_id_type=MESH).wait_recv()
    for e in range(2):
        for c in range(2):
            @pl.when(jnp.logical_not(here(e, c)))
            def _():
                copy(e, c).wait_send()

            @pl.when(here(e, c))
            def _():
                local(e, c).wait()


def exchange_audio(waves, first, mid, last, bias):
    bf16, f32 = jnp.bfloat16, jnp.float32
    return pl.pallas_call(
        audio_kernel,
        out_shape=(jax.ShapeDtypeStruct((4, 320, 128), bf16), jax.ShapeDtypeStruct((8192, 512), bf16),
                   jax.ShapeDtypeStruct((4, 128, 512), bf16), jax.ShapeDtypeStruct((7, 512), f32)),
        in_specs=[HBM, HBM, HBM, HBM, HBM],
        out_specs=(HBM, VM, VM, VM),
        scratch_shapes=[
            pltpu.VMEM((2, 40960), f32),
            pltpu.VMEM((10, 512), f32),
            pltpu.VMEM((7, 512), f32),
            pltpu.VMEM((2, 320, 128), f32),
            pltpu.VMEM((2, 320, 128), bf16),
            pltpu.VMEM((8192, 512), bf16),
            pltpu.VMEM((4, 128, 512), f32),
            pltpu.SemaphoreType.DMA((4,)),
            pltpu.SemaphoreType.DMA((4,)),
            pltpu.SemaphoreType.DMA((11,)),
        ],
        compiler_params=pltpu.CompilerParams(collective_id=1, has_side_effects=True, vmem_limit_bytes=26 << 20),
        name="audio",
    )(*[pltpu.with_memory_space_constraint(x, pltpu.HBM) for x in (
        waves, first, mid.reshape(6144, 512), last.reshape(2048, 512), bias)])


def half_gelu(h):
    h = h.astype(jnp.bfloat16)
    u = jnp.minimum(h * h, jnp.bfloat16(6.25))
    q = jnp.bfloat16(QH[3])
    for c in QH[2::-1]:
        q = q * u + jnp.bfloat16(c)
    return h + h * jnp.tanh(h * q)


def finish(v, gain, shift):
    ss = jnp.sum(v * v, axis=-1, keepdims=True)
    r = lax.rsqrt(ss * (1.0 / 512) + EPS)
    return half_gelu((v * r) * gain + shift)


class Held:
    v = None


def encoder_kernel(lens, order, utts, taps, w, bias, gain, shift, pgain, pshift, out,
                   packed, lhs, y0, y1, e1, e2, e3, e4, e5, e6, halo, out32):
    f32, bf16 = jnp.float32, jnp.bfloat16
    seq = lax.axis_index("seq")
    own, core = seq // 2, seq % 2
    packed[...] = jnp.zeros_like(packed)
    lane = lax.broadcasted_iota(jnp.int32, (320, 128), 1)
    sample = lax.broadcasted_iota(jnp.int32, (320, 128), 0) * 128 + lane
    off = jnp.int32(0)
    for p in range(4):
        u = order[own, p]
        ln = lens[own, u]
        a, b = off // 128, off % 128
        part = jnp.where(sample < ln, utts[u].astype(f32), 0.0)
        rolled = pltpu.roll(part, b, 1)
        packed[pl.ds(a, 320), :] += jnp.where(lane >= b, rolled, 0.0)
        packed[pl.ds(a + 1, 320), :] += jnp.where(lane < b, rolled, 0.0)
        off = off + ln
    nv = ((off + 10239) // 10240 - core + 1) // 2

    def row(ref, l):
        return ref[pl.ds(l, 1), :]

    def dot_(a, b):
        return jnp.dot(a, b, preferred_element_type=f32)

    def epi(y, l, groups, dst, nxt=None):
        g, s = row(gain, l) * 0.5, row(shift, l) * 0.5
        b = row(bias, l)
        for k in range(groups):
            if k % 8 == 0 and isinstance(y, Held):
                if len(y.v) <= k // 8:
                    y.v.append(y.jobs.pop(0)())
                if nxt is not None and nxt.jobs:
                    nxt.v.append(nxt.jobs.pop(0)())
            v = y.v[k // 8][16 * (k % 8):16 * (k % 8) + 16] if isinstance(y, Held) else y[pl.ds(16 * k, 16), :]
            if l > 0:
                v = v + b
            dst(k, finish(v, g, s))

    def conv3(src, l, start, rows, gap, y):
        at = 1536 * l
        if not isinstance(y, Held):
            y[pl.ds(0, rows), :] = dot_(src[pl.ds(start, rows), :], w[at:at + 1024, :]) + dot_(
                src[pl.ds(start + gap, rows), 0:512], w[at + 1024:at + 1536, :])
            return
        y.v, y.jobs = [], [lambda o=o: dot_(src[pl.ds(start + o, 128), :], w[at:at + 1024, :]) + dot_(
            src[pl.ds(start + gap + o, 128), 0:512], w[at + 1024:at + 1536, :]) for o in range(0, rows, 128)]

    def put(ref, gap, base=0):
        def at(k, v):
            ref[pl.ds((k // 2) * gap + base, 16), (k % 2) * 512:(k % 2) * 512 + 512] = v
        return at

    lane16 = lax.broadcasted_iota(jnp.int32, (16, 128), 1)
    row16 = lax.broadcasted_iota(jnp.int32, (16, 512), 0)

    def windows(cols, count):
        for q in range(count):
            j, o = divmod(20 * q, 128)
            x = cols[j] if o == 0 else pltpu.roll(cols[j], 128 - o, 1)
            if o + 25 > 128:
                x = jnp.where(lane16 < 128 - o, x, pltpu.roll(cols[j + 1], 128 - o, 1))
            x = jnp.where(lane16 >= 126, 1.0, x)
            lhs[pl.ds(16 * q, 16), :] = x.astype(bf16)

    after = packed[pl.ds(80 * core + 80, 8, stride=160), :]
    windows([jnp.concatenate([after, jnp.zeros((8, 128), f32)], axis=0)], 4)
    for v in range(4):
        y0[pl.ds(64 * v, 64), :] = dot_(lhs[0:64, :], taps[v])

    def put_first(k, val):
        ph = 4 * (k % 4) + k // 4
        e1[pl.ds(16 * (ph // 2), 16), (ph % 2) * 512:(ph % 2) * 512 + 512] = val
    epi(y0, 0, 16, put_first)
    conv3(e1, 0, 0, 112, 16, y0)
    epi(y0, 1, 7, put(e2, 16))
    conv3(e2, 1, 0, 48, 16, y0)
    epi(y0, 2, 3, put(e3, 16))
    conv3(e3, 2, 0, 16, 16, y0)

    def keep4(k, val):
        halo[48:64, :] = val.astype(f32)
    epi(y0, 3, 1, keep4)
    for k, e in enumerate((e1, e2, e3)):
        halo[16 * k:16 * k + 16, :] = e[0:16, 0:512].astype(f32)
    silent = jnp.broadcast_to(halo[56:57, :], (16, 512)).astype(bf16)

    def fill(i, _):
        for k in range(17):
            e4[pl.ds((k // 2) * 128 + 16 * i, 16), (k % 2) * 512:(k % 2) * 512 + 512] = silent
        return 0
    lax.fori_loop(nv, 8, fill, 0)

    def wrap(e, l, i, first, last):
        x = pltpu.roll(e[pl.ds(first, 16), 0:512].astype(f32), 15, 0)
        x = jnp.where(row16 == 15, halo[pl.ds(16 * l + i, 1), :], x)
        e[pl.ds(last, 16), 0:512] = x.astype(bf16)

    def segment(i, _):
        base = 5 * (32 * i + 16 * core)
        windows([packed[pl.ds(base + j, 16, stride=5), :] for j in range(6)], 32)
        y0, y1 = Held(), Held()

        def first(v, y):
            y.v, y.jobs = [], [lambda o=o: dot_(lhs[o:o + 128, :], taps[v]) for o in range(0, 512, 128)]

        def put1(v):
            def at(q, val):
                e1[pl.ds(32 * q + 16 * (v // 2), 16), 512 * (v % 2):512 * (v % 2) + 512] = val
            return at
        ys = (y0, y1)
        first(0, y0)
        for v in range(4):
            if v < 3:
                first(v + 1, ys[(v + 1) % 2])
            epi(ys[v % 2], 0, 32, put1(v), ys[(v + 1) % 2] if v < 3 else None)
        wrap(e1, 0, i, 0, 1024)
        conv3(e1, 0, 0, 256, 16, y0)
        conv3(e1, 0, 256, 256, 16, y1)
        epi(y0, 1, 16, put(e2, 16, 0), y1)
        conv3(e1, 0, 512, 256, 16, y0)
        epi(y1, 1, 16, put(e2, 16, 128), y0)
        conv3(e1, 0, 768, 256, 16, y1)
        epi(y0, 1, 16, put(e2, 16, 256), y1)
        conv3(e2, 1, 0, 256, 16, y0)
        epi(y1, 1, 16, put(e2, 16, 384), y0)
        wrap(e2, 1, i, 0, 512)
        conv3(e2, 1, 256, 256, 16, y1)
        epi(y0, 2, 16, put(e3, 16, 0), y1)
        epi(y1, 2, 16, put(e3, 16, 128))
        wrap(e3, 2, i, 0, 256)
        conv3(e3, 2, 0, 256, 16, y0)
        at = pl.multiple_of(16 * i, 16)
        epi(y0, 3, 16, put(e4, 128, at))
        wrap(e4, 3, i, at, 1024 + at)
        return 0
    lax.fori_loop(0, nv, segment, 0)

    def conv2(src, l, start, y):
        y.v, y.jobs = [], [lambda o=o: dot_(src[pl.ds(start + o, 128), :], w[6144 + 1024 * l:7168 + 1024 * l, :]) for o in (0, 128)]

    def put8(ref, base):
        def at(k, v):
            ref[pl.ds(base + 16 * (k % 8), 16), (k // 8) * 512:(k // 8) * 512 + 512] = v
        return at
    y0, y1 = Held(), Held()
    conv3(e4, 3, 0, 256, 128, y0)
    conv3(e4, 3, 256, 256, 128, y1)
    epi(y0, 4, 16, put8(e5, 0), y1)
    conv3(e4, 3, 512, 256, 128, y0)
    epi(y1, 4, 16, put8(e5, 128), y0)
    conv3(e4, 3, 768, 256, 128, y1)
    epi(y0, 4, 16, put8(e5, 256), y1)
    conv2(e5, 0, 0, y0)
    epi(y1, 4, 16, put8(e5, 384), y0)
    conv2(e5, 0, 256, y1)
    epi(y0, 5, 16, put8(e6, 0), y1)
    epi(y1, 5, 16, put8(e6, 128))
    conv2(e6, 1, 0, y0)
    pg, ps = pgain[...], pshift[...]

    def last(k, v):
        v = v.astype(f32)
        v = v - jnp.mean(v, axis=-1, keepdims=True)
        v = v * lax.rsqrt(jnp.mean(v * v, axis=-1, keepdims=True) + EPS) * pg + ps
        for c in range(4):
            out32[c, pl.ds(32 * (k % 8) + k // 8, 16, stride=2), :] = v[:, 128 * c:128 * c + 128]
    epi(y0, 6, 16, last)
    out[0:32, :] = jnp.zeros((32, 512), bf16)
    out[288:320, :] = jnp.zeros((32, 512), bf16)
    for c in range(4):
        out[32:288, 128 * c:128 * c + 128] = out32[c, 0:256, :].astype(bf16)


def encode(lens, order, utts, taps, weights, bias, gain, shift, pgain, pshift):
    bf16, f32 = jnp.bfloat16, jnp.float32
    return pl.pallas_call(
        encoder_kernel,
        out_shape=jax.ShapeDtypeStruct((320, 512), bf16),
        in_specs=[SM, SM] + [VM] * 8,
        out_specs=VM,
        scratch_shapes=[
            pltpu.VMEM((1456, 128), f32),
            pltpu.VMEM((512, 128), bf16),
            pltpu.VMEM((512, 512), f32),
            pltpu.VMEM((512, 512), f32),
            pltpu.VMEM((65 * 16, 1024), bf16),
            pltpu.VMEM((33 * 16, 1024), bf16),
            pltpu.VMEM((17 * 16, 1024), bf16),
            pltpu.VMEM((9 * 128, 1024), bf16),
            pltpu.VMEM((4 * 128, 1024), bf16),
            pltpu.VMEM((2 * 128, 1024), bf16),
            pltpu.VMEM((64, 512), f32),
            pltpu.VMEM((4, 264, 128), f32),
        ],
        compiler_params=pltpu.CompilerParams(vmem_limit_bytes=30 << 20),
        name="encode",
    )(lens, order, utts, taps, weights, bias, gain, shift, pgain, pshift)


def frames_kernel(frames, out, ssem, rsem):
    seq = lax.axis_index("seq")
    barrier = pltpu.get_barrier_semaphore()
    for o in range(1, 8):
        pl.semaphore_signal(barrier, inc=1, device_id={"seq": (seq + o) % 8}, device_id_type=MESH)

    def piece(d):
        return frames.at[pl.ds(pl.multiple_of(32 * d + 32 * (1 - seq % 2), 32), 64)]

    def copy(o):
        d = (seq + o) % 8
        return pltpu.make_async_remote_copy(
            src_ref=piece(d), dst_ref=out.at[seq], send_sem=ssem.at[o], recv_sem=rsem.at[seq],
            device_id={"seq": d}, device_id_type=MESH)
    own = pltpu.make_async_copy(piece(seq), out.at[seq], ssem.at[0])
    own.start()
    pl.semaphore_wait(barrier, 7)
    for o in range(1, 8):
        copy(o).start()
    own.wait()
    for o in range(1, 8):
        d = (seq + o) % 8
        pltpu.make_async_remote_copy(
            src_ref=piece(d), dst_ref=out.at[d], send_sem=ssem.at[o], recv_sem=rsem.at[d],
            device_id={"seq": d}, device_id_type=MESH).wait_recv()
    for o in range(1, 8):
        copy(o).wait_send()


def exchange_frames(frames):
    return pl.pallas_call(
        frames_kernel,
        out_shape=jax.ShapeDtypeStruct((8, 64, 512), jnp.bfloat16),
        in_specs=[HBM],
        out_specs=HBM,
        scratch_shapes=[pltpu.SemaphoreType.DMA((8,)), pltpu.SemaphoreType.DMA((8,))],
        compiler_params=pltpu.CompilerParams(collective_id=2, has_side_effects=True, vmem_limit_bytes=1 << 20),
        name="frames",
    )(frames)


def conformer_kernel(lens, recv, wp, pb, gain, up, taps, dbias, down, out,
                     nrm, s0, s1, lifted, ya, yb, g, act):
    f32, bf16 = jnp.float32, jnp.bfloat16
    base = 64 * lax.axis_index("seq") - 32
    for r in range(4):
        for c in range(4):
            nrm[128 * r + 32 * c:128 * r + 32 * c + 32, :] = recv[2 * r + (c + 1) % 2, 32 * (c // 2):32 * (c // 2) + 32, :]

    def dot_(a, b):
        return jnp.dot(a, b, preferred_element_type=f32)

    halves = (slice(0, 512), slice(512, 1024))
    for w in halves:
        s0[:, w] = dot_(nrm[...], wp[:, w]) + pb[:, w]

    def norm(src, l, rows):
        gl = gain[l:l + 1, :]

        def body(i, _):
            at = pl.ds(pl.multiple_of(16 * i, 16), 16)
            v = src[at, :]
            v = v - jnp.mean(v, axis=-1, keepdims=True)
            v = v * lax.rsqrt(jnp.mean(v * v, axis=-1, keepdims=True) + EPS) * gl
            lifted[at, :] = v.astype(bf16)
            return 0
        lax.fori_loop(0, rows // 16, body, 0, unroll=True)

    def module(l, per, lo, keep):
        rows = 4 * per
        first = 64 - keep // 2
        ahead = base + lo + lax.broadcasted_iota(jnp.int32, (16, 128), 0)

        def lift(n):
            ya[0:rows, :] = dot_(lifted[0:rows, :], up[l, :, 512 * n:512 * n + 512])
            yb[0:rows, :] = dot_(lifted[0:rows, :], up[l, :, 1024 + 512 * n:1536 + 512 * n])

        def gate(n):
            for r in range(4):
                total = lens[r, 0] + lens[r, 1] + lens[r, 2] + lens[r, 3]
                valid = (total - 400) // 320 + 1
                for k in range(per // 16):
                    at = slice(per * r + 16 * k, per * r + 16 * k + 16)
                    t = ahead + 16 * k
                    live = jnp.logical_and(t >= 0, t < valid)
                    for c in range(4):
                        w = slice(128 * c, 128 * c + 128)
                        v = ya[at, w] * jax.nn.sigmoid(yb[at, w])
                        g[4 * n + c, r, lo + 16 * k:lo + 16 * k + 16, :] = jnp.where(live, v, 0.0)

        def block(c, r, w):
            acc = jnp.broadcast_to(dbias[l:l + 1, w], (keep, 128))
            for j in range(31):
                acc = acc + g[c, r, first + j - 15:first + j - 15 + keep, :] * taps[j, l:l + 1, w]
            act[keep * r:keep * r + keep, w] = (acc * jax.nn.sigmoid(acc)).astype(bf16)

        def depth(c, _):
            for r in range(4):
                block(c, r, pl.ds(pl.multiple_of(128 * c, 128), 128))
            return 0
        lift(0)
        gate(0)
        lift(1)
        gate(1)
        lax.fori_loop(0, 8, depth, 0)

    norm(s0, 0, 512)
    module(0, 128, 0, 96)
    for w in halves:
        d = dot_(act[...], down[0, :, w])
        for r in range(4):
            s1[96 * r:96 * r + 96, w] = s0[128 * r + 16:128 * r + 112, w] + d[96 * r:96 * r + 96]
    norm(s1, 1, 384)
    module(1, 96, 16, 64)
    for w in halves:
        d = dot_(act[0:256, :], down[1, :, w])
        for r in range(4):
            out[r, :, w] = (s1[96 * r + 16:96 * r + 80, w] + d[64 * r:64 * r + 64]).astype(bf16)


def conform(lens, recv, wp, pb, gain, up, taps, dbias, down):
    bf16, f32 = jnp.bfloat16, jnp.float32
    return pl.pallas_call(
        conformer_kernel,
        out_shape=jax.ShapeDtypeStruct((4, 64, 1024), bf16),
        in_specs=[SM] + [VM] * 8,
        out_specs=VM,
        scratch_shapes=[
            pltpu.VMEM((512, 512), bf16),
            pltpu.VMEM((512, 1024), f32),
            pltpu.VMEM((384, 1024), f32),
            pltpu.VMEM((512, 1024), bf16),
            pltpu.VMEM((512, 512), f32),
            pltpu.VMEM((512, 512), f32),
            pltpu.VMEM((8, 4, 128, 128), f32),
            pltpu.VMEM((384, 1024), bf16),
        ],
        compiler_params=pltpu.CompilerParams(vmem_limit_bytes=20 << 20),
        name="conform",
    )(lens, recv, wp, pb, gain, up, jnp.transpose(taps, (1, 0, 2)), dbias, down)


def per_device(waveforms, utt_len, pack_order, conv_first, conv_mid, conv_last, conv_bias, conv_gain,
               conv_shift, proj_gain, proj_shift, proj_weight, proj_bias, conf_gain, conf_up,
               conf_depth, depth_bias, conf_down):
    utts, weights, taps, bias = exchange_audio(waveforms, conv_first, conv_mid, conv_last, conv_bias)
    frames = encode(utt_len, pack_order, utts, taps, weights, bias, conv_gain, conv_shift,
                    proj_gain[None], proj_shift[None])
    recv = exchange_frames(frames)
    return conform(utt_len, recv, proj_weight, proj_bias[None], conf_gain, conf_up, conf_depth,
                   depth_bias, conf_down)


def solution(mesh):
    return jax.shard_map(
        per_device,
        mesh=mesh,
        in_specs=(P(("dp", "seq"), None), P("dp", None), P("dp", None)) + (P(),) * 15,
        out_specs=P("dp", "seq", None),
        check_vma=False,
    )
```

```python
import jax
import jax.numpy as jnp
from jax import lax
from jax.experimental import pallas as pl
from jax.experimental.pallas import tpu as pltpu
from jax.sharding import PartitionSpec as P

EPS = 1e-05
QH = tuple(2.0 * c * 4.0 ** i for i, c in enumerate((0.7976911, 0.03672923, -0.00025450048, -8.666277e-06)))
MESH = pl.DeviceIdType.MESH
VM = pl.BlockSpec(memory_space=pltpu.VMEM)
SM = pl.BlockSpec(memory_space=pltpu.SMEM)
ANY = pl.BlockSpec(memory_space=pl.ANY)
HBM = pl.BlockSpec(memory_space=pltpu.HBM)


def audio_kernel(waves_in, first_in, mid, last, bias_in, out, weights, taps, bias,
                 waves, first, bias_raw, stage, held, raw, t32, ssem, rsem, wsem):
    f32, bf16 = jnp.float32, jnp.bfloat16
    dp, seq = lax.axis_index("dp"), lax.axis_index("seq")
    mine = seq == dp // 2
    barrier = pltpu.get_barrier_semaphore()

    def source(k):
        return {"dp": 4 * (seq // 2) + k, "seq": dp // 2}

    for k in range(4):
        @pl.when(jnp.logical_not(jnp.logical_and(mine, dp % 4 == k)))
        def _():
            pl.semaphore_signal(barrier, inc=1, device_id=source(k), device_id_type=MESH)

    def fetch(b):
        src = mid.at[pl.ds(1024 * b, 1024)] if b < 6 else last.at[pl.ds(1024 * (b - 6), 1024)]
        return pltpu.make_async_copy(src, raw.at[pl.ds(1024 * b, 1024)], wsem.at[b])

    small = [pltpu.make_async_copy(x, y, wsem.at[8 + k]) for k, (x, y) in enumerate(
        ((waves_in, waves), (first_in, first), (bias_in, bias_raw)))]
    for c in small:
        c.start()
    for b in range(8):
        fetch(b).start()
    small[0].wait()

    slot = dp % 4

    def copy(e, c):
        return pltpu.make_async_remote_copy(
            src_ref=held.at[e], dst_ref=out.at[slot],
            send_sem=ssem.at[2 * e + c], recv_sem=rsem.at[slot],
            device_id={"dp": 2 * seq + e, "seq": 2 * (dp // 4) + c}, device_id_type=MESH)

    def here(e, c):
        return jnp.logical_and(mine, jnp.logical_and(dp % 2 == e, seq % 2 == c))

    def local(e, c):
        return pltpu.make_async_copy(held.at[e], out.at[slot], ssem.at[2 * e + c])

    for e in range(2):
        def unfold(i, _):
            stage[e, pl.ds(i, 1), :] = waves[e:e + 1, pl.ds(pl.multiple_of(128 * i, 128), 128)]
            return 0
        lax.fori_loop(0, 320, unfold, 0, unroll=16)
        held[e] = stage[e].astype(bf16)
        if e == 0:
            pl.semaphore_wait(barrier, jnp.where(mine, 3, 4))
        for c in range(2):
            @pl.when(jnp.logical_not(here(e, c)))
            def _():
                copy(e, c).start()

            @pl.when(here(e, c))
            def _():
                local(e, c).start()

    small[1].wait()
    small[2].wait()
    b0 = bias_raw[...] - jnp.mean(bias_raw[...], axis=-1, keepdims=True)
    bias[...] = b0
    fw = first[...] - jnp.mean(first[...], axis=-1, keepdims=True)
    hi = b0[0:1].astype(bf16).astype(f32)
    t32[...] = jnp.zeros_like(t32)
    for v in range(4):
        t32[v, 5 * v:5 * v + 10, :] = fw
        t32[v, 126:127, :] = hi
        t32[v, 127:128, :] = b0[0:1] - hi
    taps[...] = t32[...].astype(bf16)
    ones = jnp.full((512, 128), 1.0 / 512, bf16)
    for b in range(8):
        fetch(b).wait()
        for i in range(4):
            at = slice(1024 * b + 256 * i, 1024 * b + 256 * i + 256)
            m = jnp.dot(raw[at, :], ones, preferred_element_type=f32)
            for c in range(4):
                k = slice(128 * c, 128 * c + 128)
                weights[at, k] = (raw[at, k].astype(f32) - m).astype(bf16)

    for k in range(4):
        @pl.when(jnp.logical_not(jnp.logical_and(mine, slot == k)))
        def _():
            pltpu.make_async_remote_copy(
                src_ref=held.at[0], dst_ref=out.at[k], send_sem=ssem.at[0], recv_sem=rsem.at[k],
                device_id=source(k), device_id_type=MESH).wait_recv()
    for e in range(2):
        for c in range(2):
            @pl.when(jnp.logical_not(here(e, c)))
            def _():
                copy(e, c).wait_send()

            @pl.when(here(e, c))
            def _():
                local(e, c).wait()


def exchange_audio(waves, first, mid, last, bias):
    bf16, f32 = jnp.bfloat16, jnp.float32
    return pl.pallas_call(
        audio_kernel,
        out_shape=(jax.ShapeDtypeStruct((4, 320, 128), bf16), jax.ShapeDtypeStruct((8192, 512), bf16),
                   jax.ShapeDtypeStruct((4, 128, 512), bf16), jax.ShapeDtypeStruct((7, 512), f32)),
        in_specs=[HBM, HBM, HBM, HBM, HBM],
        out_specs=(HBM, VM, VM, VM),
        scratch_shapes=[
            pltpu.VMEM((2, 40960), f32),
            pltpu.VMEM((10, 512), f32),
            pltpu.VMEM((7, 512), f32),
            pltpu.VMEM((2, 320, 128), f32),
            pltpu.VMEM((2, 320, 128), bf16),
            pltpu.VMEM((8192, 512), bf16),
            pltpu.VMEM((4, 128, 512), f32),
            pltpu.SemaphoreType.DMA((4,)),
            pltpu.SemaphoreType.DMA((4,)),
            pltpu.SemaphoreType.DMA((11,)),
        ],
        compiler_params=pltpu.CompilerParams(collective_id=1, has_side_effects=True, vmem_limit_bytes=26 << 20),
        name="audio",
    )(*[pltpu.with_memory_space_constraint(x, pltpu.HBM) for x in (
        waves, first, mid.reshape(6144, 512), last.reshape(2048, 512), bias)])


def half_gelu(h):
    h = h.astype(jnp.bfloat16)
    u = jnp.minimum(h * h, jnp.bfloat16(6.25))
    q = jnp.bfloat16(QH[3])
    for c in QH[2::-1]:
        q = q * u + jnp.bfloat16(c)
    return h + h * jnp.tanh(h * q)


def finish(v, gain, shift):
    ss = jnp.sum(v * v, axis=-1, keepdims=True)
    r = lax.rsqrt(ss * (1.0 / 512) + EPS)
    return half_gelu((v * r) * gain + shift)


class Held:
    v = None


def encoder_kernel(lens, order, utts, taps, w, bias, gain, shift, pgain, pshift, out,
                   packed, lhs, y0, y1, e1, e2, e3, e4, e5, e6, halo, out32):
    f32, bf16 = jnp.float32, jnp.bfloat16
    seq = lax.axis_index("seq")
    own, core = seq // 2, seq % 2
    packed[...] = jnp.zeros_like(packed)
    lane = lax.broadcasted_iota(jnp.int32, (320, 128), 1)
    sample = lax.broadcasted_iota(jnp.int32, (320, 128), 0) * 128 + lane
    off = jnp.int32(0)
    for p in range(4):
        u = order[own, p]
        ln = lens[own, u]
        a, b = off // 128, off % 128
        part = jnp.where(sample < ln, utts[u].astype(f32), 0.0)
        rolled = pltpu.roll(part, b, 1)
        packed[pl.ds(a, 320), :] += jnp.where(lane >= b, rolled, 0.0)
        packed[pl.ds(a + 1, 320), :] += jnp.where(lane < b, rolled, 0.0)
        off = off + ln
    nv = ((off + 10239) // 10240 - core + 1) // 2

    def row(ref, l):
        return ref[pl.ds(l, 1), :]

    def dot_(a, b):
        return jnp.dot(a, b, preferred_element_type=f32)

    def epi(y, l, groups, dst, nxt=None):
        g, s = row(gain, l) * 0.5, row(shift, l) * 0.5
        b = row(bias, l)
        for k in range(groups):
            if k % 8 == 0 and isinstance(y, Held):
                if len(y.v) <= k // 8:
                    y.v.append(y.jobs.pop(0)())
                if nxt is not None and nxt.jobs:
                    nxt.v.append(nxt.jobs.pop(0)())
            v = y.v[k // 8][16 * (k % 8):16 * (k % 8) + 16] if isinstance(y, Held) else y[pl.ds(16 * k, 16), :]
            if l > 0:
                v = v + b
            dst(k, finish(v, g, s))

    def conv3(src, l, start, rows, gap, y):
        at = 1536 * l
        if not isinstance(y, Held):
            y[pl.ds(0, rows), :] = dot_(src[pl.ds(start, rows), :], w[at:at + 1024, :]) + dot_(
                src[pl.ds(start + gap, rows), 0:512], w[at + 1024:at + 1536, :])
            return
        y.v, y.jobs = [], [lambda o=o: dot_(src[pl.ds(start + o, 128), :], w[at:at + 1024, :]) + dot_(
            src[pl.ds(start + gap + o, 128), 0:512], w[at + 1024:at + 1536, :]) for o in range(0, rows, 128)]

    def put(ref, gap, base=0):
        def at(k, v):
            ref[pl.ds((k // 2) * gap + base, 16), (k % 2) * 512:(k % 2) * 512 + 512] = v
        return at

    lane16 = lax.broadcasted_iota(jnp.int32, (16, 128), 1)
    row16 = lax.broadcasted_iota(jnp.int32, (16, 512), 0)

    def windows(cols, count):
        for q in range(count):
            j, o = divmod(20 * q, 128)
            x = cols[j] if o == 0 else pltpu.roll(cols[j], 128 - o, 1)
            if o + 25 > 128:
                x = jnp.where(lane16 < 128 - o, x, pltpu.roll(cols[j + 1], 128 - o, 1))
            x = jnp.where(lane16 >= 126, 1.0, x)
            lhs[pl.ds(16 * q, 16), :] = x.astype(bf16)

    after = packed[pl.ds(80 * core + 80, 8, stride=160), :]
    windows([jnp.concatenate([after, jnp.zeros((8, 128), f32)], axis=0)], 4)
    for v in range(4):
        y0[pl.ds(64 * v, 64), :] = dot_(lhs[0:64, :], taps[v])

    def put_first(k, val):
        ph = 4 * (k % 4) + k // 4
        e1[pl.ds(16 * (ph // 2), 16), (ph % 2) * 512:(ph % 2) * 512 + 512] = val
    epi(y0, 0, 16, put_first)
    conv3(e1, 0, 0, 112, 16, y0)
    epi(y0, 1, 7, put(e2, 16))
    conv3(e2, 1, 0, 48, 16, y0)
    epi(y0, 2, 3, put(e3, 16))
    conv3(e3, 2, 0, 16, 16, y0)

    def keep4(k, val):
        halo[48:64, :] = val.astype(f32)
    epi(y0, 3, 1, keep4)
    for k, e in enumerate((e1, e2, e3)):
        halo[16 * k:16 * k + 16, :] = e[0:16, 0:512].astype(f32)
    silent = jnp.broadcast_to(halo[56:57, :], (16, 512)).astype(bf16)

    def fill(i, _):
        for k in range(17):
            e4[pl.ds((k // 2) * 128 + 16 * i, 16), (k % 2) * 512:(k % 2) * 512 + 512] = silent
        return 0
    lax.fori_loop(nv, 8, fill, 0)

    def wrap(e, l, i, first, last):
        x = pltpu.roll(e[pl.ds(first, 16), 0:512].astype(f32), 15, 0)
        x = jnp.where(row16 == 15, halo[pl.ds(16 * l + i, 1), :], x)
        e[pl.ds(last, 16), 0:512] = x.astype(bf16)

    def segment(i, _):
        base = 5 * (32 * i + 16 * core)
        windows([packed[pl.ds(base + j, 16, stride=5), :] for j in range(6)], 32)
        y0, y1 = Held(), Held()

        def first(v, y):
            y.v, y.jobs = [], [lambda o=o: dot_(lhs[o:o + 128, :], taps[v]) for o in range(0, 512, 128)]

        def put1(v):
            def at(q, val):
                e1[pl.ds(32 * q + 16 * (v // 2), 16), 512 * (v % 2):512 * (v % 2) + 512] = val
            return at
        ys = (y0, y1)
        first(0, y0)
        for v in range(4):
            if v < 3:
                first(v + 1, ys[(v + 1) % 2])
            epi(ys[v % 2], 0, 32, put1(v), ys[(v + 1) % 2] if v < 3 else None)
        wrap(e1, 0, i, 0, 1024)
        conv3(e1, 0, 0, 256, 16, y0)
        conv3(e1, 0, 256, 256, 16, y1)
        epi(y0, 1, 16, put(e2, 16, 0), y1)
        conv3(e1, 0, 512, 256, 16, y0)
        epi(y1, 1, 16, put(e2, 16, 128), y0)
        conv3(e1, 0, 768, 256, 16, y1)
        epi(y0, 1, 16, put(e2, 16, 256), y1)
        conv3(e2, 1, 0, 256, 16, y0)
        epi(y1, 1, 16, put(e2, 16, 384), y0)
        wrap(e2, 1, i, 0, 512)
        conv3(e2, 1, 256, 256, 16, y1)
        epi(y0, 2, 16, put(e3, 16, 0), y1)
        epi(y1, 2, 16, put(e3, 16, 128))
        wrap(e3, 2, i, 0, 256)
        conv3(e3, 2, 0, 256, 16, y0)
        at = pl.multiple_of(16 * i, 16)
        epi(y0, 3, 16, put(e4, 128, at))
        wrap(e4, 3, i, at, 1024 + at)
        return 0
    lax.fori_loop(0, nv, segment, 0)

    def conv2(src, l, start, y):
        y.v, y.jobs = [], [lambda o=o: dot_(src[pl.ds(start + o, 128), :], w[6144 + 1024 * l:7168 + 1024 * l, :]) for o in (0, 128)]

    def put8(ref, base):
        def at(k, v):
            ref[pl.ds(base + 16 * (k % 8), 16), (k // 8) * 512:(k // 8) * 512 + 512] = v
        return at
    y0, y1 = Held(), Held()
    conv3(e4, 3, 0, 256, 128, y0)
    conv3(e4, 3, 256, 256, 128, y1)
    epi(y0, 4, 16, put8(e5, 0), y1)
    conv3(e4, 3, 512, 256, 128, y0)
    epi(y1, 4, 16, put8(e5, 128), y0)
    conv3(e4, 3, 768, 256, 128, y1)
    epi(y0, 4, 16, put8(e5, 256), y1)
    conv2(e5, 0, 0, y0)
    epi(y1, 4, 16, put8(e5, 384), y0)
    conv2(e5, 0, 256, y1)
    epi(y0, 5, 16, put8(e6, 0), y1)
    epi(y1, 5, 16, put8(e6, 128))
    conv2(e6, 1, 0, y0)
    pg, ps = pgain[...], pshift[...]

    def last(k, v):
        v = v.astype(f32)
        v = v - jnp.mean(v, axis=-1, keepdims=True)
        v = v * lax.rsqrt(jnp.mean(v * v, axis=-1, keepdims=True) + EPS) * pg + ps
        for c in range(4):
            out32[c, pl.ds(32 * (k % 8) + k // 8, 16, stride=2), :] = v[:, 128 * c:128 * c + 128]
    epi(y0, 6, 16, last)
    out[0:32, :] = jnp.zeros((32, 512), bf16)
    out[288:320, :] = jnp.zeros((32, 512), bf16)
    for c in range(4):
        out[32:288, 128 * c:128 * c + 128] = out32[c, 0:256, :].astype(bf16)


def encode(lens, order, utts, taps, weights, bias, gain, shift, pgain, pshift):
    bf16, f32 = jnp.bfloat16, jnp.float32
    return pl.pallas_call(
        encoder_kernel,
        out_shape=jax.ShapeDtypeStruct((320, 512), bf16),
        in_specs=[SM, SM] + [VM] * 8,
        out_specs=VM,
        scratch_shapes=[
            pltpu.VMEM((1456, 128), f32),
            pltpu.VMEM((512, 128), bf16),
            pltpu.VMEM((512, 512), f32),
            pltpu.VMEM((512, 512), f32),
            pltpu.VMEM((65 * 16, 1024), bf16),
            pltpu.VMEM((33 * 16, 1024), bf16),
            pltpu.VMEM((17 * 16, 1024), bf16),
            pltpu.VMEM((9 * 128, 1024), bf16),
            pltpu.VMEM((4 * 128, 1024), bf16),
            pltpu.VMEM((2 * 128, 1024), bf16),
            pltpu.VMEM((64, 512), f32),
            pltpu.VMEM((4, 264, 128), f32),
        ],
        compiler_params=pltpu.CompilerParams(vmem_limit_bytes=30 << 20),
        name="encode",
    )(lens, order, utts, taps, weights, bias, gain, shift, pgain, pshift)


def frames_kernel(frames, out, ssem, rsem):
    seq = lax.axis_index("seq")
    barrier = pltpu.get_barrier_semaphore()
    for o in range(1, 8):
        pl.semaphore_signal(barrier, inc=1, device_id={"seq": (seq + o) % 8}, device_id_type=MESH)

    def piece(d):
        return frames.at[pl.ds(pl.multiple_of(32 * d + 32 * (1 - seq % 2), 32), 64)]

    def copy(o):
        d = (seq + o) % 8
        return pltpu.make_async_remote_copy(
            src_ref=piece(d), dst_ref=out.at[seq], send_sem=ssem.at[o], recv_sem=rsem.at[seq],
            device_id={"seq": d}, device_id_type=MESH)
    own = pltpu.make_async_copy(piece(seq), out.at[seq], ssem.at[0])
    own.start()
    pl.semaphore_wait(barrier, 7)
    for o in range(1, 8):
        copy(o).start()
    own.wait()
    for o in range(1, 8):
        d = (seq + o) % 8
        pltpu.make_async_remote_copy(
            src_ref=piece(d), dst_ref=out.at[d], send_sem=ssem.at[o], recv_sem=rsem.at[d],
            device_id={"seq": d}, device_id_type=MESH).wait_recv()
    for o in range(1, 8):
        copy(o).wait_send()


def exchange_frames(frames):
    return pl.pallas_call(
        frames_kernel,
        out_shape=jax.ShapeDtypeStruct((8, 64, 512), jnp.bfloat16),
        in_specs=[HBM],
        out_specs=HBM,
        scratch_shapes=[pltpu.SemaphoreType.DMA((8,)), pltpu.SemaphoreType.DMA((8,))],
        compiler_params=pltpu.CompilerParams(collective_id=2, has_side_effects=True, vmem_limit_bytes=1 << 20),
        name="frames",
    )(frames)


def conformer_kernel(lens, recv, wp, pb, gain, up, taps, dbias, down, out,
                     nrm, s0, s1, lifted, ya, yb, g, act):
    f32, bf16 = jnp.float32, jnp.bfloat16
    base = 64 * lax.axis_index("seq") - 32
    for r in range(4):
        for c in range(4):
            nrm[128 * r + 32 * c:128 * r + 32 * c + 32, :] = recv[2 * r + (c + 1) % 2, 32 * (c // 2):32 * (c // 2) + 32, :]

    def dot_(a, b):
        return jnp.dot(a, b, preferred_element_type=f32)

    halves = (slice(0, 512), slice(512, 1024))
    for w in halves:
        s0[:, w] = dot_(nrm[...], wp[:, w]) + pb[:, w]

    def norm(src, l, rows):
        gl = gain[l:l + 1, :]

        def body(i, _):
            at = pl.ds(pl.multiple_of(16 * i, 16), 16)
            v = src[at, :]
            v = v - jnp.mean(v, axis=-1, keepdims=True)
            v = v * lax.rsqrt(jnp.mean(v * v, axis=-1, keepdims=True) + EPS) * gl
            lifted[at, :] = v.astype(bf16)
            return 0
        lax.fori_loop(0, rows // 16, body, 0, unroll=True)

    def module(l, per, lo, keep):
        rows = 4 * per
        first = 64 - keep // 2
        ahead = base + lo + lax.broadcasted_iota(jnp.int32, (16, 128), 0)

        def lift(n):
            ya[0:rows, :] = dot_(lifted[0:rows, :], up[l, :, 512 * n:512 * n + 512])
            yb[0:rows, :] = dot_(lifted[0:rows, :], up[l, :, 1024 + 512 * n:1536 + 512 * n])

        def gate(n):
            for r in range(4):
                total = lens[r, 0] + lens[r, 1] + lens[r, 2] + lens[r, 3]
                valid = (total - 400) // 320 + 1
                for k in range(per // 16):
                    at = slice(per * r + 16 * k, per * r + 16 * k + 16)
                    t = ahead + 16 * k
                    live = jnp.logical_and(t >= 0, t < valid)
                    for c in range(4):
                        w = slice(128 * c, 128 * c + 128)
                        v = ya[at, w] * jax.nn.sigmoid(yb[at, w])
                        g[4 * n + c, r, lo + 16 * k:lo + 16 * k + 16, :] = jnp.where(live, v, 0.0)

        def block(c, r, w):
            acc = jnp.broadcast_to(dbias[l:l + 1, w], (keep, 128))
            for j in range(31):
                acc = acc + g[c, r, first + j - 15:first + j - 15 + keep, :] * taps[j, l:l + 1, w]
            act[keep * r:keep * r + keep, w] = (acc * jax.nn.sigmoid(acc)).astype(bf16)

        def depth(c, _):
            for r in range(4):
                block(c, r, pl.ds(pl.multiple_of(128 * c, 128), 128))
            return 0
        lift(0)
        gate(0)
        lift(1)
        gate(1)
        lax.fori_loop(0, 8, depth, 0)

    norm(s0, 0, 512)
    module(0, 128, 0, 96)
    for w in halves:
        d = dot_(act[...], down[0, :, w])
        for r in range(4):
            s1[96 * r:96 * r + 96, w] = s0[128 * r + 16:128 * r + 112, w] + d[96 * r:96 * r + 96]
    norm(s1, 1, 384)
    module(1, 96, 16, 64)
    for w in halves:
        d = dot_(act[0:256, :], down[1, :, w])
        for r in range(4):
            out[r, :, w] = (s1[96 * r + 16:96 * r + 80, w] + d[64 * r:64 * r + 64]).astype(bf16)


def conform(lens, recv, wp, pb, gain, up, taps, dbias, down):
    bf16, f32 = jnp.bfloat16, jnp.float32
    return pl.pallas_call(
        conformer_kernel,
        out_shape=jax.ShapeDtypeStruct((4, 64, 1024), bf16),
        in_specs=[SM] + [VM] * 8,
        out_specs=VM,
        scratch_shapes=[
            pltpu.VMEM((512, 512), bf16),
            pltpu.VMEM((512, 1024), f32),
            pltpu.VMEM((384, 1024), f32),
            pltpu.VMEM((512, 1024), bf16),
            pltpu.VMEM((512, 512), f32),
            pltpu.VMEM((512, 512), f32),
            pltpu.VMEM((8, 4, 128, 128), f32),
            pltpu.VMEM((384, 1024), bf16),
        ],
        compiler_params=pltpu.CompilerParams(vmem_limit_bytes=20 << 20),
        name="conform",
    )(lens, recv, wp, pb, gain, up, jnp.transpose(taps, (1, 0, 2)), dbias, down)


def per_device(waveforms, utt_len, pack_order, conv_first, conv_mid, conv_last, conv_bias, conv_gain,
               conv_shift, proj_gain, proj_shift, proj_weight, proj_bias, conf_gain, conf_up,
               conf_depth, depth_bias, conf_down):
    utts, weights, taps, bias = exchange_audio(waveforms, conv_first, conv_mid, conv_last, conv_bias)
    frames = encode(utt_len, pack_order, utts, taps, weights, bias, conv_gain, conv_shift,
                    proj_gain[None], proj_shift[None])
    recv = exchange_frames(frames)
    return conform(utt_len, recv, proj_weight, proj_bias[None], conf_gain, conf_up, conf_depth,
                   depth_bias, conf_down)


def solution(mesh):
    return jax.shard_map(
        per_device,
        mesh=mesh,
        in_specs=(P(("dp", "seq"), None), P("dp", None), P("dp", None)) + (P(),) * 15,
        out_specs=P("dp", "seq", None),
        check_vma=False,
    )
```
